256 devices in a mesh: group: 8 (over z), ghost: 32 (over x, y, core).
Axes of the slice: x: 4, y: 4, z: 8, core: 2. Of those that a mesh axis runs over, the one named last changes fastest.
Arguments:
- inputs: bfloat16 [200704, 1024], P(('group', 'ghost')), may hold values from -24 to 24
- out_grad: bfloat16 [200704, 1024], P(('group', 'ghost')), may hold values from -6 to 6
- conv_first: bfloat16 [1024, 256], replicated, may hold values from -0.25 to 0.25
- conv_middle: bfloat16 [2304, 256], replicated, may hold values from -0.1875 to 0.1875
- conv_last: bfloat16 [256, 1024], replicated, may hold values from -0.375 to 0.375
- gain: float32 [1024], replicated, may hold values from 0.5 to 1.5
Outputs:
- input_grad: bfloat16 [200704, 1024], P(('group', 'ghost'))
- first_grad: float32 [262144], P(('group', 'ghost'))
- middle_grad: float32 [589824], P(('group', 'ghost'))
- last_grad: float32 [262144], P(('group', 'ghost'))
- gain_grad: float32 [1024], P(('group', 'ghost'))
The draws below stay inside these ranges and needn't reach their ends.
All inputs are finite; a program needn't handle non-finite values.
Results may differ from the reference program's by a relative error of at most 0.0071.
Values sent between devices are 32-bit elements; how exact they have to be, the bound alone decides.
A program may use at most 128 MiB of HBM per device.

```python
import jax
import jax.numpy as jnp
from jax import lax

WIDE = 1024
MID = 256
GROUP = 64
NEWTON = 5
SIDE = 14
GHOST_ROWS = 25088
CELLS = 200704


def raised(array, rng, source, target, blocks, factor):
    def block_of(axis_at):
        return (jnp.arange(array.shape[axis_at]) // (array.shape[axis_at] // blocks)).reshape((-1,) + (1,) * (array.ndim - 1 - axis_at))

    first = jax.random.permutation(rng, blocks)[block_of(target)]
    far = (block_of(target) + blocks // 2) % blocks
    return jnp.where((block_of(source) == first) | (block_of(source) == far), factor * array, array)


def shard_levels(stream_key, extent, shards, smallest, top_value):
    def one(position, blocks):
        draws = jax.random.uniform(jax.random.fold_in(jax.random.fold_in(stream_key, 6), position), (blocks,), jnp.float32, smallest / len(shards), top_value / len(shards))
        return jnp.repeat(jnp.exp(draws), extent[position] // blocks).reshape((-1,) + (1,) * (len(extent) - position - 1))

    loudness = one(*shards[0])
    for cut in shards[1:]:
        loudness = loudness * one(*cut)
    return loudness


def normal_values(rng, dims, width, bound, cuts=(), held_as=jnp.bfloat16):
    loudness = shard_levels(rng, dims, cuts, -0.22, 0.18) if cuts else 1.0
    drawn = jax.random.normal(rng, dims, jnp.float32) * width * loudness
    return jnp.minimum(jnp.maximum(drawn, -bound), bound).astype(held_as)


def heavy_noise(stream_key, dims, scale, most, cuts, heavy, kind=jnp.bfloat16):
    entries = scale * jax.random.normal(stream_key, dims, jnp.float32)
    if cuts:
        entries = entries * shard_levels(stream_key, dims, cuts, -0.22, 0.18)
    return jnp.clip(raised(entries, jax.random.fold_in(stream_key, 3), *heavy), -most, most).astype(kind)


def setup_inputs(seed: int = 0) -> dict:
    streams_of = jax.random.split(jax.random.key(seed), 7)
    inputs = heavy_noise(streams_of[0], (CELLS, WIDE), 1.0, 24.0, ((0, 256),), (0, 1, 256, 6.0))
    out_grad = normal_values(streams_of[1], (CELLS, WIDE), 1.0, 6.0, ((0, 256),))
    conv_first = normal_values(streams_of[2], (WIDE, MID), (WIDE / 2) ** -0.5, 0.25)
    conv_middle = normal_values(streams_of[3], (9 * MID, MID), (9 * MID / 2) ** -0.5, 0.1875)
    conv_last = normal_values(streams_of[4], (MID, WIDE), MID ** -0.5, 0.375)
    gain = jnp.clip(1.0 + 0.1 * jax.random.normal(streams_of[5], (WIDE,), jnp.float32), 0.5, 1.5)
    return dict(inputs=inputs, out_grad=out_grad, conv_first=conv_first, conv_middle=conv_middle, conv_last=conv_last, gain=gain)


epsilon = 1e-05

def silu_slope(value):
    sig = jax.nn.sigmoid(value)
    return sig * (1.0 + value * (1.0 - sig))

def patches(act, side):
    channels = act.shape[-1]
    images = act.reshape(-1, side, side, channels)
    padded = jnp.pad(images, ((0, 0), (1, 1), (1, 1), (0, 0)))
    pieces = [padded[:, row_off:row_off + side, col_off:col_off + side, :] for row_off in range(3) for col_off in range(3)]
    return jnp.concatenate(pieces, axis=-1).reshape(-1, 9 * channels)

def unpatch(dcolumns, side):
    channels = dcolumns.shape[-1] // 9
    images = dcolumns.reshape(-1, side, side, 9, channels)
    padded = jnp.pad(images, ((0, 0), (1, 1), (1, 1), (0, 0), (0, 0)))
    summed = jnp.zeros((images.shape[0], side, side, channels), jnp.float32)
    for row_off in range(3):
        for col_off in range(3):
            summed = summed + padded[:, 2 - row_off:2 - row_off + side, 2 - col_off:2 - col_off + side, 3 * row_off + col_off, :]
    return summed.reshape(-1, channels)

def batched(left, right):
    return jnp.einsum('gij,gjk->gik', left, right, precision=lax.Precision.HIGHEST)

def gram(left, right):
    return jnp.einsum('rgi,rgj->gij', left, right, precision=lax.Precision.HIGHEST)

def whitener(covariance):
    traces = jnp.trace(covariance, axis1=1, axis2=2)
    normed = covariance / traces[:, None, None]
    identity = jnp.broadcast_to(jnp.eye(covariance.shape[1], dtype=jnp.float32), covariance.shape)
    project = identity
    for sweep in range(NEWTON):
        cubed = batched(batched(project, project), project)
        project = 1.5 * project - 0.5 * batched(cubed, normed)
    return project / jnp.sqrt(traces)[:, None, None]

def contract(left, right):
    return lax.dot_general(left, right, (((0,), (0,)), ((), ())), preferred_element_type=jnp.float32)

def ghost_pass(inputs, out_grad, conv_first, conv_middle, conv_last, gain):
    rows = inputs.shape[0]
    blocks = WIDE // GROUP
    act1 = jnp.dot(inputs, conv_first, preferred_element_type=jnp.float32)
    hidden1 = jax.nn.silu(act1).astype(jnp.bfloat16)
    columns = patches(hidden1, SIDE)
    act2 = jnp.dot(columns, conv_middle, preferred_element_type=jnp.float32)
    hidden2 = jax.nn.silu(act2).astype(jnp.bfloat16)
    branch = jnp.dot(hidden2, conv_last, preferred_element_type=jnp.float32)
    mean = lax.optimization_barrier(jnp.sum(branch, 0)) / rows
    centered = branch - mean
    grouped = centered.reshape(rows, blocks, GROUP)
    identity = jnp.broadcast_to(jnp.eye(GROUP, dtype=jnp.float32), (blocks, GROUP, GROUP))
    covariance = gram(grouped, grouped) / rows + epsilon * identity
    whiten, pullback = jax.vjp(whitener, covariance)
    white = jnp.einsum('rgi,gij->rgj', grouped, whiten, precision=lax.Precision.HIGHEST).reshape(rows, WIDE)
    pre = inputs.astype(jnp.float32) + gain * white
    dpre = out_grad.astype(jnp.float32) * silu_slope(pre)
    dwhite = (dpre * gain).reshape(rows, blocks, GROUP)
    gain_part = lax.optimization_barrier(jnp.sum(dpre * white, 0))
    colsum = lax.optimization_barrier(jnp.sum(dwhite, 0))
    cross = gram(grouped, dwhite)
    dcov = pullback(cross)[0]
    sym_cov = dcov + jnp.swapaxes(dcov, 1, 2)
    dbranch = jnp.einsum('rgj,gij->rgi', dwhite - colsum / rows, whiten, precision=lax.Precision.HIGHEST)
    dbranch = dbranch + jnp.einsum('rgi,gij->rgj', grouped, sym_cov, precision=lax.Precision.HIGHEST) / rows
    dbranch = dbranch.reshape(rows, WIDE).astype(jnp.bfloat16)
    last_part = contract(hidden2, dbranch)
    dmid2 = (lax.dot_general(dbranch, conv_last, (((1,), (1,)), ((), ())), preferred_element_type=jnp.float32) * silu_slope(act2)).astype(jnp.bfloat16)
    middle_part = contract(columns, dmid2)
    dcolumns = lax.dot_general(dmid2, conv_middle, (((1,), (1,)), ((), ())), preferred_element_type=jnp.float32)
    dhid1 = unpatch(dcolumns, SIDE)
    dmid1 = (dhid1 * silu_slope(act1)).astype(jnp.bfloat16)
    first_part = contract(inputs, dmid1)
    input_grad = (lax.dot_general(dmid1, conv_first, (((1,), (1,)), ((), ())), preferred_element_type=jnp.float32) + dpre).astype(jnp.bfloat16)
    return (input_grad, (first_part, middle_part, last_part, gain_part))

def reference(inputs, out_grad, conv_first, conv_middle, conv_last, gain):
    count = CELLS // GHOST_ROWS
    xs_in = inputs.reshape(count, GHOST_ROWS, WIDE)
    xs_grad = out_grad.reshape(count, GHOST_ROWS, WIDE)
    start = (jnp.zeros((WIDE, MID), jnp.float32), jnp.zeros((9 * MID, MID), jnp.float32), jnp.zeros((MID, WIDE), jnp.float32), jnp.zeros((WIDE,), jnp.float32))

    def step_fn(carry, pieces):
        result, parts = ghost_pass(pieces[0], pieces[1], conv_first, conv_middle, conv_last, gain)
        return (jax.tree.map(lambda left, right: left + right, carry, parts), result)
    sums, grads = lax.scan(step_fn, start, (xs_in, xs_grad))
    scale = CELLS ** (-0.5)
    return (grads.reshape(CELLS, WIDE), (sums[0] * scale).reshape(-1), (sums[1] * scale).reshape(-1), (sums[2] * scale).reshape(-1), sums[3] * scale)
```

```python
import jax
import jax.numpy as jnp
from jax import lax
from jax.experimental import pallas as pl
from jax.experimental.pallas import tpu as pltpu
from jax.sharding import PartitionSpec as P

GROUP = 64
NEWTON = 5
SIDE = 14
PAD = 16
TILE = 112
MESH = pl.DeviceIdType.MESH
epsilon = 1e-05
F32 = jnp.float32
BF16 = jnp.bfloat16


def dot(left, right, dims=((1,), (0,))):
    return lax.dot_general(left, right, (dims, ((), ())), preferred_element_type=F32)


def parts(value, count):
    pieces = []
    for _ in range(count):
        piece = value.astype(BF16)
        pieces.append(piece)
        value = value - piece.astype(F32)
    return pieces


def dot_parts(left, right, dims=((1,), (0,))):
    total = None
    for a in left:
        for b in right:
            term = dot(a, b, dims)
            total = term if total is None else total + term
    return total


def dot_high(left, right, dims=((1,), (0,))):
    return lax.dot_general(
        left, right, (dims, ((), ())), preferred_element_type=F32, precision=lax.Precision.HIGHEST
    )


def tile_rows(t):
    return pl.ds(pl.multiple_of(t * TILE, TILE), TILE)


def fold(block, right):
    top, low = block[:32], block[32:]
    lane = lax.broadcasted_iota(jnp.int32, (32, 128), 1)
    if right:
        top = pltpu.roll(top, 64, 1)
    else:
        low = pltpu.roll(low, 64, 1)
    return jnp.where(lane < 64, top, low)


def unfold(folded, right):
    lane = lax.broadcasted_iota(jnp.int32, (32, 128), 1)
    other = pltpu.roll(folded, 64, 1)
    top, low = (other, folded) if right else (folded, other)
    keep = (lane >= 64) if right else (lane < 64)
    return jnp.where(keep, top, 0.0), jnp.where(keep, low, 0.0)


def fill_diagonal(target, source):
    target[...] = jnp.zeros_like(target)
    for k in range(16):
        j, at = k // 4, (k % 4) * GROUP
        lanes = slice((at // 128) * 128, (at // 128) * 128 + 128)
        top, low = unfold(source[k, :32, :], bool(k % 2))
        target[j, at : at + 32, lanes] = top
        target[j, at + 32 : at + 64, lanes] = low


def fill_row(target, source):
    lane = lax.broadcasted_iota(jnp.int32, (8, 128), 1)
    for pair in range(8):
        left = source[2 * pair, 32:40, :]
        right = pltpu.roll(source[2 * pair + 1, 32:40, :], 64, 1)
        target[:, pair * 128 : pair * 128 + 128] = jnp.where(lane < 64, left, right)


def pack_row(row, k):
    piece = row[:, (k // 2) * 128 : (k // 2) * 128 + 128]
    return pltpu.roll(piece, 64, 1) if k % 2 else piece


def edges(t):
    row = lax.broadcasted_iota(jnp.int32, (TILE, 256), 0).astype(F32) + float(t * TILE)
    line = jnp.floor((row + 0.5) * (1.0 / SIDE))
    column = row - line * SIDE
    image = jnp.floor((line + 0.5) * (1.0 / SIDE))
    return line - image * SIDE, column


def shifted_tiles(padded, columns, sign):
    for t in range(columns.shape[0] // TILE):
        line, column = edges(t)
        at = slice(t * TILE, t * TILE + TILE)
        for tap in range(9):
            dr, dc = sign * (tap // 3 - 1), sign * (tap % 3 - 1)
            start = t * TILE + PAD + dr * SIDE + dc
            value = padded[start : start + TILE, :]
            keep = None
            if dr:
                keep = line > 0.5 if dr < 0 else line < SIDE - 1.5
            if dc:
                side = column > 0.5 if dc < 0 else column < SIDE - 1.5
                keep = side if keep is None else keep & side
            if keep is not None:
                value = jnp.where(keep, value, 0.0)
            columns[at, tap * 256 : tap * 256 + 256] = value.astype(BF16)


def forward_kernel(x, a, b, c, h1, s1, h2, s2, gram, hsum, payload, acc, padded, columns, wide):
    rows = x.shape[0]
    acc[...] = dot(x[...], a[...])
    padded[:PAD, :] = jnp.zeros((PAD, 256), F32)
    padded[rows + PAD :, :] = jnp.zeros((PAD, 256), F32)

    def first(t, carry):
        v = acc[tile_rows(t), :]
        s = 1.0 / (1.0 + jnp.exp(-v))
        s1[tile_rows(t), :] = s * (1.0 + v * (1.0 - s))
        h = (v * s).astype(BF16)
        h1[tile_rows(t), :] = h
        padded[pl.ds(t * TILE + PAD, TILE), :] = h.astype(F32)
        return carry

    lax.fori_loop(0, rows // TILE, first, 0)
    shifted_tiles(padded, columns, 1)
    acc[...] = dot(columns[...], b[...])

    def second(t, carry):
        v = acc[tile_rows(t), :]
        s = 1.0 / (1.0 + jnp.exp(-v))
        s2[tile_rows(t), :] = s * (1.0 + v * (1.0 - s))
        h2[tile_rows(t), :] = (v * s).astype(BF16)
        return carry

    lax.fori_loop(0, rows // TILE, second, 0)
    h = h2[...]
    gram[...] = dot(h, h, ((0,), (0,)))
    hsum[...] = dot(h, jnp.ones((rows, 128), BF16), ((0,), (0,)))
    wide[...] = dot_parts(parts(gram[...], 3), [c[...]])
    row = dot(jnp.ones((8, rows), BF16), h)
    brow = dot_parts(parts(row, 3), [c[...]])
    for j in range(4):
        here = slice(j * 256, j * 256 + 256)
        square = dot_parts([c[:, here]], parts(wide[:, here], 3), ((0,), (0,)))
        for q in range(4):
            k = 4 * j + q
            lanes = slice((q // 2) * 128, (q // 2) * 128 + 128)
            payload[k, :32, :] = fold(square[q * 64 : q * 64 + 64, lanes], bool(q % 2))
            payload[k, 32:40, :] = pack_row(brow, k)


def middle_kernel(whites, h2, x, og, gain, c, dpre, dwhite, d, across, gains, payload, diagonal, offset, white, csum):
    rows = x.shape[0]
    fill_diagonal(diagonal, whites)
    fill_row(offset, whites)
    for j in range(4):
        here = slice(j * 256, j * 256 + 256)
        folded = dot_parts([c[:, here]], parts(diagonal[j], 2))
        high, low = parts(folded, 2)
        d[:, here] = high
        white[:, here] = dot(h2[...], high) + dot(h2[...], low)
    csum[...] = jnp.zeros_like(csum)
    gains[...] = jnp.zeros_like(gains)

    def body(t, carry):
        for j in range(8):
            here = slice(j * 128, j * 128 + 128)
            w = white[tile_rows(t), here] - offset[0:1, here]
            g = gain[0:1, here]
            v = x[tile_rows(t), here].astype(F32) + g * w
            s = 1.0 / (1.0 + jnp.exp(-v))
            u = og[tile_rows(t), here].astype(F32) * (s * (1.0 + v * (1.0 - s)))
            dpre[tile_rows(t), here] = u
            dw = g * u
            dwhite[tile_rows(t), here] = dw.astype(BF16)
            csum[:, here] += jnp.sum(dw.reshape(TILE // 8, 8, 128), axis=0)
            gains[:, here] += jnp.sum((u * w).reshape(TILE // 8, 8, 128), axis=0)
        return carry

    lax.fori_loop(0, rows // TILE, body, 0)
    across[...] = dot(h2[...], dwhite[...], ((0,), (0,)))
    total = jnp.broadcast_to(jnp.sum(csum[...], axis=0, keepdims=True), (8, csum.shape[1]))
    for j in range(4):
        here = slice(j * 256, j * 256 + 256)
        square = dot_parts([c[:, here]], parts(across[:, here], 2), ((0,), (0,)))
        for q in range(4):
            k = 4 * j + q
            lanes = slice((q // 2) * 128, (q // 2) * 128 + 128)
            payload[k, :32, :] = fold(square[q * 64 : q * 64 + 64, lanes], bool(q % 2))
            payload[k, 32:40, :] = pack_row(total, k)


def backward_kernel(
    span, slopes, whites, x, a, b, c, h1, s1, h2, s2, gram, hsum, dpre, dwhite, d, across, gains,
    input_grad, grads, acc, padded, columns, diagonal, e, last, mid, top, row,
):
    rows = x.shape[0]
    fill_diagonal(diagonal, slopes)
    fill_row(row, slopes)
    for j in range(4):
        here = slice(j * 256, j * 256 + 256)
        e[:, here] = (dot_parts([c[:, here]], parts(diagonal[j], 2)) * (1.0 / span)).astype(BF16)
    back = dot(e[...], c[...], ((1,), (1,))).astype(BF16)
    const = dot_parts(parts(row[...], 2), [c[...]], ((1,), (1,)))
    acc[...] = dot(dwhite[...], d[...], ((1,), (1,))) + dot(h2[...], back)
    padded[:PAD, :] = jnp.zeros((PAD, 256), F32)
    padded[rows + PAD :, :] = jnp.zeros((PAD, 256), F32)

    def second(t, carry):
        v = (acc[tile_rows(t), :] - const[0:1, :]) * s2[tile_rows(t), :]
        padded[pl.ds(t * TILE + PAD, TILE), :] = v.astype(BF16).astype(F32)
        return carry

    lax.fori_loop(0, rows // TILE, second, 0)
    shifted_tiles(padded, columns, -1)
    for tap in range(9):
        here = slice(tap * 256, tap * 256 + 256)
        term = dot(columns[:, here], b[here, :], ((1,), (1,)))
        if tap == 0:
            acc[...] = term
        else:
            acc[...] += term
        value = dot(h1[...], columns[:, here], ((0,), (0,)))
        for half in range(2):
            mid[half, here, :] = value[:, half * 128 : half * 128 + 128]

    def first(t, carry):
        padded[pl.ds(t * TILE + PAD, TILE), :] = acc[tile_rows(t), :] * s1[tile_rows(t), :]
        return carry

    lax.fori_loop(0, rows // TILE, first, 0)
    dmid1 = padded[PAD : rows + PAD, :].astype(BF16)
    value = dot(x[...], dmid1, ((0,), (0,)))
    for half in range(2):
        top[half] = value[:, half * 128 : half * 128 + 128]
    for j in range(4):
        here = slice(j * 256, j * 256 + 256)
        input_grad[:, here] = (dot(dmid1, a[here, :], ((1,), (1,))) + dpre[:, here]).astype(BF16)
    fill_diagonal(diagonal, whites)
    grams = parts(gram[...], 2)
    for j in range(4):
        here = slice(j * 256, j * 256 + 256)
        high, low = parts(across[:, here], 2)
        white = parts(diagonal[j], 2)
        value = dot_parts([high], white, ((1,), (1,))) + dot(low, white[0], ((1,), (1,)))
        last[:, here] = value + dot_parts(grams, [e[:, here]])
    for j in range(8):
        here = slice(j * 128, j * 128 + 128)
        grads[:, 3328 + j * 128 : 3456 + j * 128] = last[:, here] - hsum[...] * row[0:1, here]
    for half in range(2):
        for q in range(4):
            at = q * 256 + half * 128
            grads[:, at : at + 128] = top[half, pl.ds(q, 256, stride=4), :]
        for q in range(9):
            at = 1024 + q * 256 + half * 128
            grads[:, at : at + 128] = mid[half, pl.ds(q, 256, stride=9), :]
    total = jnp.sum(gains[...], axis=0, keepdims=True)
    own = lax.broadcasted_iota(jnp.int32, (256, 1024), 0)
    channel = lax.broadcasted_iota(jnp.int32, (256, 1024), 1)
    spread = jnp.where((channel >> 2) == own, total, 0.0)
    channel = lax.broadcasted_iota(jnp.int32, (1024, 128), 0)
    lane = lax.broadcasted_iota(jnp.int32, (1024, 128), 1)
    pick = jnp.where((channel & 3) == lane, 1.0, 0.0).astype(BF16)
    grads[:, 4352:4480] = dot_parts(parts(spread, 3), [pick])


def newton(n, size):
    row = lax.broadcasted_iota(jnp.int32, (size, size), 0)
    lane = lax.broadcasted_iota(jnp.int32, (size, size), 1)
    project = jnp.where(row == lane, 1.5, 0.0) - 0.5 * n
    for sweep in range(NEWTON - 1):
        squared = dot_high(project, project)
        project = 1.5 * project - 0.5 * dot_high(squared, dot_high(project, n))
    return project


def trace_of(block, size=64):
    row = lax.broadcasted_iota(jnp.int32, (size, size), 0)
    lane = lax.broadcasted_iota(jnp.int32, (size, size), 1)
    return jnp.sum(jnp.where(row == lane, block, 0.0))


def square_of(folded):
    return jnp.concatenate([folded[:32, :64], pltpu.roll(folded[:32], 64, 1)[:, :64]], axis=0)


def folded_of(square):
    return jnp.concatenate([square[:32], square[32:]], axis=1)


def whiten_block(total, span):
    row64 = total[32:40, :64] * (1.0 / span)
    outer = dot_high(jnp.where(lax.broadcasted_iota(jnp.int32, (8, 64), 0) == 0, row64, 0.0), row64, ((0,), (0,)))
    r = lax.broadcasted_iota(jnp.int32, (64, 64), 0)
    c = lax.broadcasted_iota(jnp.int32, (64, 64), 1)
    cov = square_of(total) * (1.0 / span) - outer + jnp.where(r == c, epsilon, 0.0)
    trace = trace_of(cov)
    scaled = cov / trace
    white = newton(scaled, 64) / jnp.sqrt(jnp.full((64, 64), trace))
    offset = dot_high(row64, white)
    return cov, white, row64, offset


def slope_block(total, cov, white, mean, span):
    csum = total[32:40, :64]
    outer = dot_high(jnp.where(lax.broadcasted_iota(jnp.int32, (8, 64), 0) == 0, mean, 0.0), csum, ((0,), (0,)))
    cross = square_of(total) - outer
    trace = trace_of(cov)
    root = jnp.sqrt(jnp.full((64, 64), trace))
    scaled = cov / trace
    up = jnp.concatenate([scaled, cross / root], axis=1)
    low = jnp.concatenate([jnp.zeros((64, 64), F32), scaled], axis=1)
    project = newton(jnp.concatenate([up, low], axis=0), 128)
    dn = project[:64, 64:]
    dt = -jnp.sum(dn * scaled) / trace - 0.5 * jnp.sum(cross * white) / trace
    r = lax.broadcasted_iota(jnp.int32, (64, 64), 0)
    c = lax.broadcasted_iota(jnp.int32, (64, 64), 1)
    dcov = dn / trace + jnp.where(r == c, dt, 0.0)
    sym = dcov + dcov.T
    line = (dot_high(csum, white, ((1,), (1,))) + dot_high(mean, sym)) * (1.0 / span)
    return sym, line


def ghost_device(group, chip, core):
    return (group, chip * 2 + core)


def exchange_kernel(solve, payload, state, out, keep, got, part, other, mine, sems):
    group, ghost = lax.axis_index("group"), lax.axis_index("ghost")
    chip, core = ghost // 2, ghost % 2
    send, recv, send_back, recv_back, pair = sems
    barrier = pltpu.get_barrier_semaphore()

    def greet(s, carry):
        peer = ghost_device(group, (chip + s) % 16, core)
        pl.semaphore_signal(barrier, inc=1, device_id=peer, device_id_type=MESH)
        return carry

    lax.fori_loop(1, 16, greet, 0)
    partner = ghost_device(group, chip, 1 - core)
    pl.semaphore_signal(barrier, inc=1, device_id=partner, device_id_type=MESH)
    pl.semaphore_wait(barrier, 16)

    def scatter(s):
        target = (chip + s) % 16
        return pltpu.make_async_remote_copy(
            src_ref=payload.at[target], dst_ref=got.at[s], send_sem=send.at[s], recv_sem=recv.at[s],
            device_id=ghost_device(group, target, core), device_id_type=MESH,
        )

    def start(s, carry):
        scatter(s).start()
        return carry

    lax.fori_loop(1, 16, start, 0)
    part[...] = payload[chip]

    def add(s, carry):
        scatter(s).wait_recv()
        part[...] += got[s]
        return carry

    lax.fori_loop(1, 16, add, 0)
    swap = pltpu.make_async_remote_copy(
        src_ref=part, dst_ref=other, send_sem=pair.at[0], recv_sem=pair.at[1],
        device_id=partner, device_id_type=MESH,
    )
    swap.start()
    swap.wait_recv()
    solve(part[...] + other[...], state, mine, keep)
    out[chip] = mine[...]

    def spread(s):
        return pltpu.make_async_remote_copy(
            src_ref=mine, dst_ref=out.at[chip], send_sem=send_back.at[s], recv_sem=recv_back.at[s],
            device_id=ghost_device(group, (chip + s) % 16, core), device_id_type=MESH,
        )

    def arrival(s):
        return pltpu.make_async_remote_copy(
            src_ref=mine, dst_ref=out.at[(chip + 16 - s) % 16], send_sem=send_back.at[s],
            recv_sem=recv_back.at[s], device_id=ghost_device(group, (chip + s) % 16, core), device_id_type=MESH,
        )

    def start_back(s, carry):
        spread(s).start()
        return carry

    lax.fori_loop(1, 16, start_back, 0)

    def finish(s, carry):
        arrival(s).wait_recv()
        return carry

    lax.fori_loop(1, 16, finish, 0)

    def drain(s, carry):
        scatter(s).wait_send()
        spread(s).wait_send()
        return carry

    lax.fori_loop(1, 16, drain, 0)
    swap.wait_send()


def solve_white(span, total, state, mine, keep):
    cov, white, mean, offset = whiten_block(total, span)
    keep[:64] = cov
    keep[64:128] = white
    keep[128:136] = mean
    mine[:32, :] = folded_of(white)
    mine[32:40, :] = jnp.concatenate([offset, offset], axis=1)


def solve_slope(span, total, state, mine, keep):
    sym, line = slope_block(total, state[:64], state[64:128], state[128:136], span)
    keep[...] = jnp.zeros_like(keep)
    mine[:32, :] = folded_of(sym)
    mine[32:40, :] = jnp.concatenate([line, line], axis=1)


VM = pl.BlockSpec(memory_space=pltpu.VMEM)
LIMIT = pltpu.CompilerParams(vmem_limit_bytes=60 * 1024 * 1024)


def shape(dims, kind=F32):
    return jax.ShapeDtypeStruct(dims, kind)


def exchange(payload, state, span, solve, number, name):
    def body(payload, state, out, keep, got, part, other, mine, *sems):
        exchange_kernel(
            lambda *args: solve(span, *args), payload, state, out, keep, got, part, other, mine, sems
        )

    dma = pltpu.SemaphoreType.DMA
    return pl.pallas_call(
        body,
        out_shape=(shape((16, 40, 128)), shape((136, 64))),
        in_specs=[VM] * 2,
        out_specs=[VM] * 2,
        scratch_shapes=[
            pltpu.VMEM((16, 40, 128), F32),
            pltpu.VMEM((40, 128), F32),
            pltpu.VMEM((40, 128), F32),
            pltpu.VMEM((40, 128), F32),
            dma((16,)), dma((16,)), dma((16,)), dma((16,)), dma((2,)),
        ],
        compiler_params=pltpu.CompilerParams(collective_id=number, has_side_effects=True),
        name=name,
    )(payload, state)


def forward(x, a, b, c):
    rows = x.shape[0]
    return pl.pallas_call(
        forward_kernel,
        out_shape=(
            shape((rows, 256), BF16), shape((rows, 256)), shape((rows, 256), BF16), shape((rows, 256)),
            shape((256, 256)), shape((256, 128)), shape((16, 40, 128)),
        ),
        in_specs=[VM] * 4,
        out_specs=[VM] * 7,
        scratch_shapes=[
            pltpu.VMEM((rows, 256), F32),
            pltpu.VMEM((rows + 2 * PAD, 256), F32),
            pltpu.VMEM((rows, 2304), BF16),
            pltpu.VMEM((256, 1024), F32),
        ],
        compiler_params=LIMIT,
        name="forward",
    )(x, a, b, c)


def middle(whites, h2, x, og, gain, c):
    rows = x.shape[0]
    return pl.pallas_call(
        middle_kernel,
        out_shape=(
            shape((rows, 1024)), shape((rows, 1024), BF16), shape((256, 1024), BF16), shape((256, 1024)),
            shape((8, 1024)), shape((16, 40, 128)),
        ),
        in_specs=[VM] * 6,
        out_specs=[VM] * 6,
        scratch_shapes=[
            pltpu.VMEM((4, 256, 256), F32),
            pltpu.VMEM((8, 1024), F32),
            pltpu.VMEM((rows, 1024), F32),
            pltpu.VMEM((8, 1024), F32),
        ],
        compiler_params=LIMIT,
        name="middle",
    )(whites, h2, x, og, gain, c)


def backward(span, *args):
    rows = args[2].shape[0]

    def body(*refs):
        backward_kernel(span, *refs)

    return pl.pallas_call(
        body,
        out_shape=(shape((rows, 1024), BF16), shape((256, 4480))),
        in_specs=[VM] * len(args),
        out_specs=[VM] * 2,
        scratch_shapes=[
            pltpu.VMEM((rows, 256), F32),
            pltpu.VMEM((rows + 2 * PAD, 256), F32),
            pltpu.VMEM((rows, 2304), BF16),
            pltpu.VMEM((4, 256, 256), F32),
            pltpu.VMEM((256, 1024), BF16),
            pltpu.VMEM((256, 1024), F32),
            pltpu.VMEM((2, 2304, 128), F32),
            pltpu.VMEM((2, 1024, 128), F32),
            pltpu.VMEM((8, 1024), F32),
        ],
        compiler_params=LIMIT,
        name="backward",
    )(*args)


def shards(inputs, out_grad, conv_first, conv_middle, conv_last, gain):
    ghosts, groups = lax.axis_size("ghost"), lax.axis_size("group")
    span = float(inputs.shape[0] * ghosts)
    h1, s1, h2, s2, gram, hsum, payload = forward(inputs, conv_first, conv_middle, conv_last)
    whites, state = exchange(payload, jnp.zeros((136, 64), F32), span, solve_white, 0, "whiten")
    dpre, dwhite, d, across, gains, payload = middle(
        whites, h2, inputs, out_grad, gain.reshape(1, -1), conv_last
    )
    slopes, _ = exchange(payload, state, span, solve_slope, 1, "slope")
    input_grad, grads = backward(
        span, slopes, whites, inputs, conv_first, conv_middle, conv_last, h1, s1, h2, s2, gram, hsum,
        dpre, dwhite, d, across, gains,
    )
    grads = lax.psum_scatter(grads, ("group", "ghost"), scatter_dimension=0, tiled=True)
    grads = grads.reshape(-1) * (span * groups) ** (-0.5)
    return input_grad, grads[:1024], grads[1024:3328], grads[3328:4352], grads[4352:4356]


def solution(mesh):
    rows = P(("group", "ghost"))
    return jax.shard_map(
        shards,
        mesh=mesh,
        in_specs=(P(("group", "ghost"), None), P(("group", "ghost"), None), P(), P(), P(), P()),
        out_specs=(P(("group", "ghost"), None), rows, rows, rows, rows),
        check_vma=False,
    )
```

```python
import jax
import jax.numpy as jnp
from jax import lax
from jax.experimental import pallas as pl
from jax.experimental.pallas import tpu as pltpu
from jax.sharding import PartitionSpec as P

GROUP = 64
NEWTON = 5
SIDE = 14
PAD = 16
TILE = 112
MESH = pl.DeviceIdType.MESH
epsilon = 1e-05
F32 = jnp.float32
BF16 = jnp.bfloat16


def dot(left, right, dims=((1,), (0,))):
    return lax.dot_general(left, right, (dims, ((), ())), preferred_element_type=F32)


def parts(value, count):
    pieces = []
    for _ in range(count):
        piece = value.astype(BF16)
        pieces.append(piece)
        value = value - piece.astype(F32)
    return pieces


def dot_parts(left, right, dims=((1,), (0,))):
    total = None
    for a in left:
        for b in right:
            term = dot(a, b, dims)
            total = term if total is None else total + term
    return total


def dot_high(left, right, dims=((1,), (0,))):
    return lax.dot_general(
        left, right, (dims, ((), ())), preferred_element_type=F32, precision=lax.Precision.HIGHEST
    )


def tile_rows(t):
    return pl.ds(pl.multiple_of(t * TILE, TILE), TILE)


def fold(block, right):
    top, low = block[:32], block[32:]
    lane = lax.broadcasted_iota(jnp.int32, (32, 128), 1)
    if right:
        top = pltpu.roll(top, 64, 1)
    else:
        low = pltpu.roll(low, 64, 1)
    return jnp.where(lane < 64, top, low)


def unfold(folded, right):
    lane = lax.broadcasted_iota(jnp.int32, (32, 128), 1)
    other = pltpu.roll(folded, 64, 1)
    top, low = (other, folded) if right else (folded, other)
    keep = (lane >= 64) if right else (lane < 64)
    return jnp.where(keep, top, 0.0), jnp.where(keep, low, 0.0)


def fill_diagonal(target, source):
    target[...] = jnp.zeros_like(target)
    for k in range(16):
        j, at = k // 4, (k % 4) * GROUP
        lanes = slice((at // 128) * 128, (at // 128) * 128 + 128)
        top, low = unfold(source[k, :32, :], bool(k % 2))
        target[j, at : at + 32, lanes] = top
        target[j, at + 32 : at + 64, lanes] = low


def fill_row(target, source):
    lane = lax.broadcasted_iota(jnp.int32, (8, 128), 1)
    for pair in range(8):
        left = source[2 * pair, 32:40, :]
        right = pltpu.roll(source[2 * pair + 1, 32:40, :], 64, 1)
        target[:, pair * 128 : pair * 128 + 128] = jnp.where(lane < 64, left, right)


def pack_row(row, k):
    piece = row[:, (k // 2) * 128 : (k // 2) * 128 + 128]
    return pltpu.roll(piece, 64, 1) if k % 2 else piece


def edges(t):
    row = lax.broadcasted_iota(jnp.int32, (TILE, 256), 0).astype(F32) + float(t * TILE)
    line = jnp.floor((row + 0.5) * (1.0 / SIDE))
    column = row - line * SIDE
    image = jnp.floor((line + 0.5) * (1.0 / SIDE))
    return line - image * SIDE, column


def shifted_tiles(padded, columns, sign):
    for t in range(columns.shape[0] // TILE):
        line, column = edges(t)
        at = slice(t * TILE, t * TILE + TILE)
        for tap in range(9):
            dr, dc = sign * (tap // 3 - 1), sign * (tap % 3 - 1)
            start = t * TILE + PAD + dr * SIDE + dc
            value = padded[start : start + TILE, :]
            keep = None
            if dr:
                keep = line > 0.5 if dr < 0 else line < SIDE - 1.5
            if dc:
                side = column > 0.5 if dc < 0 else column < SIDE - 1.5
                keep = side if keep is None else keep & side
            if keep is not None:
                value = jnp.where(keep, value, 0.0)
            columns[at, tap * 256 : tap * 256 + 256] = value.astype(BF16)


def forward_kernel(x, a, b, c, h1, s1, h2, s2, gram, hsum, payload, acc, padded, columns, wide):
    rows = x.shape[0]
    acc[...] = dot(x[...], a[...])
    padded[:PAD, :] = jnp.zeros((PAD, 256), F32)
    padded[rows + PAD :, :] = jnp.zeros((PAD, 256), F32)

    def first(t, carry):
        v = acc[tile_rows(t), :]
        s = 1.0 / (1.0 + jnp.exp(-v))
        s1[tile_rows(t), :] = s * (1.0 + v * (1.0 - s))
        h = (v * s).astype(BF16)
        h1[tile_rows(t), :] = h
        padded[pl.ds(t * TILE + PAD, TILE), :] = h.astype(F32)
        return carry

    lax.fori_loop(0, rows // TILE, first, 0)
    shifted_tiles(padded, columns, 1)
    acc[...] = dot(columns[...], b[...])

    def second(t, carry):
        v = acc[tile_rows(t), :]
        s = 1.0 / (1.0 + jnp.exp(-v))
        s2[tile_rows(t), :] = s * (1.0 + v * (1.0 - s))
        h2[tile_rows(t), :] = (v * s).astype(BF16)
        return carry

    lax.fori_loop(0, rows // TILE, second, 0)
    h = h2[...]
    gram[...] = dot(h, h, ((0,), (0,)))
    hsum[...] = dot(h, jnp.ones((rows, 128), BF16), ((0,), (0,)))
    wide[...] = dot_parts(parts(gram[...], 3), [c[...]])
    row = dot(jnp.ones((8, rows), BF16), h)
    brow = dot_parts(parts(row, 3), [c[...]])
    for j in range(4):
        here = slice(j * 256, j * 256 + 256)
        square = dot_parts([c[:, here]], parts(wide[:, here], 3), ((0,), (0,)))
        for q in range(4):
            k = 4 * j + q
            lanes = slice((q // 2) * 128, (q // 2) * 128 + 128)
            payload[k, :32, :] = fold(square[q * 64 : q * 64 + 64, lanes], bool(q % 2))
            payload[k, 32:40, :] = pack_row(brow, k)


def middle_kernel(whites, h2, x, og, gain, c, dpre, dwhite, d, across, gains, payload, diagonal, offset, white, csum):
    rows = x.shape[0]
    fill_diagonal(diagonal, whites)
    fill_row(offset, whites)
    for j in range(4):
        here = slice(j * 256, j * 256 + 256)
        folded = dot_parts([c[:, here]], parts(diagonal[j], 2))
        high, low = parts(folded, 2)
        d[:, here] = high
        white[:, here] = dot(h2[...], high) + dot(h2[...], low)
    csum[...] = jnp.zeros_like(csum)
    gains[...] = jnp.zeros_like(gains)

    def body(t, carry):
        for j in range(8):
            here = slice(j * 128, j * 128 + 128)
            w = white[tile_rows(t), here] - offset[0:1, here]
            g = gain[0:1, here]
            v = x[tile_rows(t), here].astype(F32) + g * w
            s = 1.0 / (1.0 + jnp.exp(-v))
            u = og[tile_rows(t), here].astype(F32) * (s * (1.0 + v * (1.0 - s)))
            dpre[tile_rows(t), here] = u
            dw = g * u
            dwhite[tile_rows(t), here] = dw.astype(BF16)
            csum[:, here] += jnp.sum(dw.reshape(TILE // 8, 8, 128), axis=0)
            gains[:, here] += jnp.sum((u * w).reshape(TILE // 8, 8, 128), axis=0)
        return carry

    lax.fori_loop(0, rows // TILE, body, 0)
    across[...] = dot(h2[...], dwhite[...], ((0,), (0,)))
    total = jnp.broadcast_to(jnp.sum(csum[...], axis=0, keepdims=True), (8, csum.shape[1]))
    for j in range(4):
        here = slice(j * 256, j * 256 + 256)
        square = dot_parts([c[:, here]], parts(across[:, here], 2), ((0,), (0,)))
        for q in range(4):
            k = 4 * j + q
            lanes = slice((q // 2) * 128, (q // 2) * 128 + 128)
            payload[k, :32, :] = fold(square[q * 64 : q * 64 + 64, lanes], bool(q % 2))
            payload[k, 32:40, :] = pack_row(total, k)


def backward_kernel(
    span, slopes, whites, x, a, b, c, h1, s1, h2, s2, gram, hsum, dpre, dwhite, d, across, gains,
    input_grad, grads, acc, padded, columns, diagonal, e, last, mid, top, row,
):
    rows = x.shape[0]
    fill_diagonal(diagonal, slopes)
    fill_row(row, slopes)
    for j in range(4):
        here = slice(j * 256, j * 256 + 256)
        e[:, here] = (dot_parts([c[:, here]], parts(diagonal[j], 2)) * (1.0 / span)).astype(BF16)
    back = dot(e[...], c[...], ((1,), (1,))).astype(BF16)
    const = dot_parts(parts(row[...], 2), [c[...]], ((1,), (1,)))
    acc[...] = dot(dwhite[...], d[...], ((1,), (1,))) + dot(h2[...], back)
    padded[:PAD, :] = jnp.zeros((PAD, 256), F32)
    padded[rows + PAD :, :] = jnp.zeros((PAD, 256), F32)

    def second(t, carry):
        v = (acc[tile_rows(t), :] - const[0:1, :]) * s2[tile_rows(t), :]
        padded[pl.ds(t * TILE + PAD, TILE), :] = v.astype(BF16).astype(F32)
        return carry

    lax.fori_loop(0, rows // TILE, second, 0)
    shifted_tiles(padded, columns, -1)
    for tap in range(9):
        here = slice(tap * 256, tap * 256 + 256)
        term = dot(columns[:, here], b[here, :], ((1,), (1,)))
        if tap == 0:
            acc[...] = term
        else:
            acc[...] += term
        value = dot(h1[...], columns[:, here], ((0,), (0,)))
        for half in range(2):
            mid[half, here, :] = value[:, half * 128 : half * 128 + 128]

    def first(t, carry):
        padded[pl.ds(t * TILE + PAD, TILE), :] = acc[tile_rows(t), :] * s1[tile_rows(t), :]
        return carry

    lax.fori_loop(0, rows // TILE, first, 0)
    dmid1 = padded[PAD : rows + PAD, :].astype(BF16)
    value = dot(x[...], dmid1, ((0,), (0,)))
    for half in range(2):
        top[half] = value[:, half * 128 : half * 128 + 128]
    for j in range(4):
        here = slice(j * 256, j * 256 + 256)
        input_grad[:, here] = (dot(dmid1, a[here, :], ((1,), (1,))) + dpre[:, here]).astype(BF16)
    fill_diagonal(diagonal, whites)
    grams = parts(gram[...], 2)
    for j in range(4):
        here = slice(j * 256, j * 256 + 256)
        high, low = parts(across[:, here], 2)
        white = parts(diagonal[j], 2)
        value = dot_parts([high], white, ((1,), (1,))) + dot(low, white[0], ((1,), (1,)))
        value = value + dot_parts(grams, [e[:, here]])
        for half in range(2):
            last[2 * j + half] = value[:, half * 128 : half * 128 + 128]
    for j in range(8):
        here = slice(j * 128, j * 128 + 128)
        last[j] = last[j] - hsum[...] * row[0:1, here]
    pack_grads(grads, top, mid, last, gains)


SLOTS = 40


def slot_rows(core, slot):
    return pl.ds(core * 128 * SLOTS + slot, 128, stride=SLOTS)


def pack_grads(grads, top, mid, last, gains):
    for core in range(2):
        for j in range(8):
            grads[slot_rows(core, j), :] = last[j, pl.ds(core, 128, stride=2), :]
        for half in range(2):
            for q in range(9):
                grads[slot_rows(core, 8 + 2 * q + half), :] = mid[half, pl.ds(q + 9 * core, 128, stride=18), :]
            for q in range(4):
                grads[slot_rows(core, 32 + 2 * q + half), :] = top[half, pl.ds(q + 4 * core, 128, stride=8), :]
    total = jnp.sum(gains[...], axis=0, keepdims=True)
    row = lax.broadcasted_iota(jnp.int32, (256, 1024), 0)
    own = (row & 127) * 2 + (row >> 7)
    channel = lax.broadcasted_iota(jnp.int32, (256, 1024), 1)
    spread = jnp.where((channel >> 2) == own, total, 0.0)
    channel = lax.broadcasted_iota(jnp.int32, (1024, 128), 0)
    lane = lax.broadcasted_iota(jnp.int32, (1024, 128), 1)
    pick = jnp.where((channel & 3) == lane, 1.0, 0.0).astype(BF16)
    value = dot_parts(parts(spread, 3), [pick])
    for core in range(2):
        grads[slot_rows(core, 26), :] = value[core * 128 : core * 128 + 128]
        for slot in range(27, 32):
            grads[slot_rows(core, slot), :] = jnp.zeros((128, 128), F32)


def scatter_kernel(scale, grads, out, other, total, wide_a, wide_b, thin_a, thin_b, half_a, half_b, last, sems):
    z, ghost = lax.axis_index("group"), lax.axis_index("ghost")
    x, y, core = ghost // 8, (ghost // 2) % 4, ghost % 2

    def device(z, x, y, core):
        return (z, x * 8 + y * 2 + core)

    partner = device(z, x, y, 1 - core)
    xs = [device(z, (x + s) % 4, y, core) for s in range(4)]
    ys = [device(z, x, (y + s) % 4, core) for s in range(4)]
    zs = [device((z + s) % 8, x, y, core) for s in range(8)]
    barrier = pltpu.get_barrier_semaphore()
    for peer in [partner] + xs[1:] + ys[1:] + zs[1:]:
        pl.semaphore_signal(barrier, inc=1, device_id=peer, device_id_type=MESH)
    pl.semaphore_wait(barrier, 14)
    send, recv = sems

    def copy(source, target, at, peer):
        return pltpu.make_async_remote_copy(
            src_ref=source, dst_ref=target, send_sem=send.at[at], recv_sem=recv.at[at],
            device_id=peer, device_id_type=MESH,
        )

    swaps = [copy(grads.at[1 - core, 4 * h : 4 * h + 4], other.at[4 * h : 4 * h + 4], h, partner) for h in range(2)]
    for swap in swaps:
        swap.start()
    first_a = [copy(total.at[0:4, (x + s) % 4], wide_a.at[s], 4 + s, xs[s]) for s in range(1, 4)]
    first_b = [copy(total.at[4:8, :, (y + s) % 4], wide_b.at[s], 8 + s, ys[s]) for s in range(1, 4)]
    for h, group in enumerate((first_a, first_b)):
        swaps[h].wait_recv()

        def join(i, carry):
            total[4 * h + i] = grads[core, 4 * h + i] + other[4 * h + i]
            return carry

        lax.fori_loop(0, 4, join, 0)
        for one in group:
            one.start()
    then_a = [copy(half_a.at[:, (y + s) % 4], thin_a.at[s], 12 + s, ys[s]) for s in range(1, 4)]
    then_b = [copy(half_b.at[:, (x + s) % 4], thin_b.at[s], 16 + s, xs[s]) for s in range(1, 4)]
    for one in first_a:
        one.wait_recv()
    for i in range(4):
        half_a[i] = total[i, x] + wide_a[1, i] + wide_a[2, i] + wide_a[3, i]
    for one in then_a:
        one.start()
    for one in first_b:
        one.wait_recv()
    for i in range(4):
        half_b[i] = total[4 + i, :, y] + wide_b[1, i] + wide_b[2, i] + wide_b[3, i]
    for one in then_b:
        one.start()
    final = [copy(other.at[(z + s) % 8, 0, 0], last.at[s], 20 + s, zs[s]) for s in range(1, 8)]
    for one in then_a:
        one.wait_recv()
    for i in range(4):
        other[i, 0, 0] = half_a[i, y] + thin_a[1, i] + thin_a[2, i] + thin_a[3, i]
    for one in then_b:
        one.wait_recv()
    for i in range(4):
        other[4 + i, 0, 0] = half_b[i, x] + thin_b[1, i] + thin_b[2, i] + thin_b[3, i]
    for one in final:
        one.start()
    result = other[z, 0, 0]
    for s in range(1, 8):
        final[s - 1].wait_recv()
        result = result + last[s]
    out[...] = result * scale
    for one in swaps + first_a + first_b + then_a + then_b + final:
        one.wait_send()


def newton(n, size):
    row = lax.broadcasted_iota(jnp.int32, (size, size), 0)
    lane = lax.broadcasted_iota(jnp.int32, (size, size), 1)
    project = jnp.where(row == lane, 1.5, 0.0) - 0.5 * n
    for sweep in range(NEWTON - 1):
        squared = dot_high(project, project)
        project = 1.5 * project - 0.5 * dot_high(squared, dot_high(project, n))
    return project


def trace_of(block, size=64):
    row = lax.broadcasted_iota(jnp.int32, (size, size), 0)
    lane = lax.broadcasted_iota(jnp.int32, (size, size), 1)
    return jnp.sum(jnp.where(row == lane, block, 0.0))


def square_of(folded):
    return jnp.concatenate([folded[:32, :64], pltpu.roll(folded[:32], 64, 1)[:, :64]], axis=0)


def folded_of(square):
    return jnp.concatenate([square[:32], square[32:]], axis=1)


def whiten_block(total, span):
    row64 = total[32:40, :64] * (1.0 / span)
    outer = dot_high(jnp.where(lax.broadcasted_iota(jnp.int32, (8, 64), 0) == 0, row64, 0.0), row64, ((0,), (0,)))
    r = lax.broadcasted_iota(jnp.int32, (64, 64), 0)
    c = lax.broadcasted_iota(jnp.int32, (64, 64), 1)
    cov = square_of(total) * (1.0 / span) - outer + jnp.where(r == c, epsilon, 0.0)
    trace = trace_of(cov)
    scaled = cov / trace
    white = newton(scaled, 64) / jnp.sqrt(jnp.full((64, 64), trace))
    offset = dot_high(row64, white)
    return cov, white, row64, offset


def slope_block(total, cov, white, mean, span):
    csum = total[32:40, :64]
    outer = dot_high(jnp.where(lax.broadcasted_iota(jnp.int32, (8, 64), 0) == 0, mean, 0.0), csum, ((0,), (0,)))
    cross = square_of(total) - outer
    trace = trace_of(cov)
    root = jnp.sqrt(jnp.full((64, 64), trace))
    scaled = cov / trace
    up = jnp.concatenate([scaled, cross / root], axis=1)
    low = jnp.concatenate([jnp.zeros((64, 64), F32), scaled], axis=1)
    project = newton(jnp.concatenate([up, low], axis=0), 128)
    dn = project[:64, 64:]
    dt = -jnp.sum(dn * scaled) / trace - 0.5 * jnp.sum(cross * white) / trace
    r = lax.broadcasted_iota(jnp.int32, (64, 64), 0)
    c = lax.broadcasted_iota(jnp.int32, (64, 64), 1)
    dcov = dn / trace + jnp.where(r == c, dt, 0.0)
    sym = dcov + dcov.T
    line = (dot_high(csum, white, ((1,), (1,))) + dot_high(mean, sym)) * (1.0 / span)
    return sym, line


def ghost_device(group, chip, core):
    return (group, chip * 2 + core)


def exchange_kernel(solve, payload, state, out, keep, got, part, other, mine, sems):
    group, ghost = lax.axis_index("group"), lax.axis_index("ghost")
    chip, core = ghost // 2, ghost % 2
    send, recv, send_back, recv_back, pair = sems
    barrier = pltpu.get_barrier_semaphore()

    def greet(s, carry):
        peer = ghost_device(group, (chip + s) % 16, core)
        pl.semaphore_signal(barrier, inc=1, device_id=peer, device_id_type=MESH)
        return carry

    lax.fori_loop(1, 16, greet, 0)
    partner = ghost_device(group, chip, 1 - core)
    pl.semaphore_signal(barrier, inc=1, device_id=partner, device_id_type=MESH)
    pl.semaphore_wait(barrier, 16)

    def scatter(s):
        target = (chip + s) % 16
        return pltpu.make_async_remote_copy(
            src_ref=payload.at[target], dst_ref=got.at[s], send_sem=send.at[s], recv_sem=recv.at[s],
            device_id=ghost_device(group, target, core), device_id_type=MESH,
        )

    def start(s, carry):
        scatter(s).start()
        return carry

    lax.fori_loop(1, 16, start, 0)
    part[...] = payload[chip]

    def add(s, carry):
        scatter(s).wait_recv()
        part[...] += got[s]
        return carry

    lax.fori_loop(1, 16, add, 0)
    swap = pltpu.make_async_remote_copy(
        src_ref=part, dst_ref=other, send_sem=pair.at[0], recv_sem=pair.at[1],
        device_id=partner, device_id_type=MESH,
    )
    swap.start()
    swap.wait_recv()
    solve(part[...] + other[...], state, mine, keep)
    out[chip] = mine[...]

    def spread(s):
        return pltpu.make_async_remote_copy(
            src_ref=mine, dst_ref=out.at[chip], send_sem=send_back.at[s], recv_sem=recv_back.at[s],
            device_id=ghost_device(group, (chip + s) % 16, core), device_id_type=MESH,
        )

    def arrival(s):
        return pltpu.make_async_remote_copy(
            src_ref=mine, dst_ref=out.at[(chip + 16 - s) % 16], send_sem=send_back.at[s],
            recv_sem=recv_back.at[s], device_id=ghost_device(group, (chip + s) % 16, core), device_id_type=MESH,
        )

    def start_back(s, carry):
        spread(s).start()
        return carry

    lax.fori_loop(1, 16, start_back, 0)

    def finish(s, carry):
        arrival(s).wait_recv()
        return carry

    lax.fori_loop(1, 16, finish, 0)

    def drain(s, carry):
        scatter(s).wait_send()
        spread(s).wait_send()
        return carry

    lax.fori_loop(1, 16, drain, 0)
    swap.wait_send()


def solve_white(span, total, state, mine, keep):
    cov, white, mean, offset = whiten_block(total, span)
    keep[:64] = cov
    keep[64:128] = white
    keep[128:136] = mean
    mine[:32, :] = folded_of(white)
    mine[32:40, :] = jnp.concatenate([offset, offset], axis=1)


def solve_slope(span, total, state, mine, keep):
    sym, line = slope_block(total, state[:64], state[64:128], state[128:136], span)
    keep[...] = jnp.zeros_like(keep)
    mine[:32, :] = folded_of(sym)
    mine[32:40, :] = jnp.concatenate([line, line], axis=1)


VM = pl.BlockSpec(memory_space=pltpu.VMEM)
LIMIT = pltpu.CompilerParams(vmem_limit_bytes=60 * 1024 * 1024)


def shape(dims, kind=F32):
    return jax.ShapeDtypeStruct(dims, kind)


def exchange(payload, state, span, solve, number, name):
    def body(payload, state, out, keep, got, part, other, mine, *sems):
        exchange_kernel(
            lambda *args: solve(span, *args), payload, state, out, keep, got, part, other, mine, sems
        )

    dma = pltpu.SemaphoreType.DMA
    return pl.pallas_call(
        body,
        out_shape=(shape((16, 40, 128)), shape((136, 64))),
        in_specs=[VM] * 2,
        out_specs=[VM] * 2,
        scratch_shapes=[
            pltpu.VMEM((16, 40, 128), F32),
            pltpu.VMEM((40, 128), F32),
            pltpu.VMEM((40, 128), F32),
            pltpu.VMEM((40, 128), F32),
            dma((16,)), dma((16,)), dma((16,)), dma((16,)), dma((2,)),
        ],
        compiler_params=pltpu.CompilerParams(collective_id=number, has_side_effects=True),
        name=name,
    )(payload, state)


def forward(x, a, b, c):
    rows = x.shape[0]
    return pl.pallas_call(
        forward_kernel,
        out_shape=(
            shape((rows, 256), BF16), shape((rows, 256)), shape((rows, 256), BF16), shape((rows, 256)),
            shape((256, 256)), shape((256, 128)), shape((16, 40, 128)),
        ),
        in_specs=[VM] * 4,
        out_specs=[VM] * 7,
        scratch_shapes=[
            pltpu.VMEM((rows, 256), F32),
            pltpu.VMEM((rows + 2 * PAD, 256), F32),
            pltpu.VMEM((rows, 2304), BF16),
            pltpu.VMEM((256, 1024), F32),
        ],
        compiler_params=LIMIT,
        name="forward",
    )(x, a, b, c)


def middle(whites, h2, x, og, gain, c):
    rows = x.shape[0]
    return pl.pallas_call(
        middle_kernel,
        out_shape=(
            shape((rows, 1024)), shape((rows, 1024), BF16), shape((256, 1024), BF16), shape((256, 1024)),
            shape((8, 1024)), shape((16, 40, 128)),
        ),
        in_specs=[VM] * 6,
        out_specs=[VM] * 6,
        scratch_shapes=[
            pltpu.VMEM((4, 256, 256), F32),
            pltpu.VMEM((8, 1024), F32),
            pltpu.VMEM((rows, 1024), F32),
            pltpu.VMEM((8, 1024), F32),
        ],
        compiler_params=LIMIT,
        name="middle",
    )(whites, h2, x, og, gain, c)


def backward(span, *args):
    rows = args[2].shape[0]

    def body(*refs):
        backward_kernel(span, *refs)

    return pl.pallas_call(
        body,
        out_shape=(shape((rows, 1024), BF16), shape((256 * SLOTS, 128))),
        in_specs=[VM] * len(args),
        out_specs=[VM] * 2,
        scratch_shapes=[
            pltpu.VMEM((rows, 256), F32),
            pltpu.VMEM((rows + 2 * PAD, 256), F32),
            pltpu.VMEM((rows, 2304), BF16),
            pltpu.VMEM((4, 256, 256), F32),
            pltpu.VMEM((256, 1024), BF16),
            pltpu.VMEM((8, 256, 128), F32),
            pltpu.VMEM((2, 2304, 128), F32),
            pltpu.VMEM((2, 1024, 128), F32),
            pltpu.VMEM((8, 1024), F32),
        ],
        compiler_params=LIMIT,
        name="backward",
    )(*args)


def scatter(grads, scale):
    def body(grads, out, other, total, wide_a, wide_b, thin_a, thin_b, half_a, half_b, last, *sems):
        scatter_kernel(
            scale, grads, out, other, total, wide_a, wide_b, thin_a, thin_b, half_a, half_b, last, sems
        )

    dma = pltpu.SemaphoreType.DMA
    return pl.pallas_call(
        body,
        out_shape=shape((SLOTS, 128)),
        in_specs=[VM],
        out_specs=VM,
        scratch_shapes=[
            pltpu.VMEM((8, 4, 4, SLOTS, 128), F32),
            pltpu.VMEM((8, 4, 4, SLOTS, 128), F32),
            pltpu.VMEM((4, 4, 4, SLOTS, 128), F32),
            pltpu.VMEM((4, 4, 4, SLOTS, 128), F32),
            pltpu.VMEM((4, 4, SLOTS, 128), F32),
            pltpu.VMEM((4, 4, SLOTS, 128), F32),
            pltpu.VMEM((4, 4, SLOTS, 128), F32),
            pltpu.VMEM((4, 4, SLOTS, 128), F32),
            pltpu.VMEM((8, SLOTS, 128), F32),
            dma((28,)), dma((28,)),
        ],
        compiler_params=pltpu.CompilerParams(
            collective_id=2, has_side_effects=True, vmem_limit_bytes=60 * 1024 * 1024
        ),
        name="scatter",
    )(grads)


def shards(inputs, out_grad, conv_first, conv_middle, conv_last, gain):
    ghosts, groups = lax.axis_size("ghost"), lax.axis_size("group")
    span = float(inputs.shape[0] * ghosts)
    h1, s1, h2, s2, gram, hsum, payload = forward(inputs, conv_first, conv_middle, conv_last)
    whites, state = exchange(payload, jnp.zeros((136, 64), F32), span, solve_white, 0, "whiten")
    dpre, dwhite, d, across, gains, payload = middle(
        whites, h2, inputs, out_grad, gain.reshape(1, -1), conv_last
    )
    slopes, _ = exchange(payload, state, span, solve_slope, 1, "slope")
    input_grad, grads = backward(
        span, slopes, whites, inputs, conv_first, conv_middle, conv_last, h1, s1, h2, s2, gram, hsum,
        dpre, dwhite, d, across, gains,
    )
    sums = scatter(grads.reshape(2, 8, 4, 4, SLOTS, 128), (span * groups) ** (-0.5))
    return (
        input_grad, sums[32:40].reshape(-1), sums[8:26].reshape(-1), sums[0:8].reshape(-1), sums[26, :4]
    )


def solution(mesh):
    rows = P(("group", "ghost"))
    return jax.shard_map(
        shards,
        mesh=mesh,
        in_specs=(P(("group", "ghost"), None), P(("group", "ghost"), None), P(), P(), P(), P()),
        out_specs=(P(("group", "ghost"), None), rows, rows, rows, rows),
        check_vma=False,
    )
```

```python
import jax
import jax.numpy as jnp
from jax import lax
from jax.experimental import pallas as pl
from jax.experimental.pallas import tpu as pltpu
from jax.sharding import PartitionSpec as P

GROUP = 64
NEWTON = 5
SIDE = 14
PAD = 16
TILE = 112
MESH = pl.DeviceIdType.MESH
epsilon = 1e-05
F32 = jnp.float32
BF16 = jnp.bfloat16


def dot(left, right, dims=((1,), (0,))):
    return lax.dot_general(left, right, (dims, ((), ())), preferred_element_type=F32)


def parts(value, count):
    pieces = []
    for _ in range(count):
        piece = value.astype(BF16)
        pieces.append(piece)
        value = value - piece.astype(F32)
    return pieces


def dot_parts(left, right, dims=((1,), (0,))):
    total = None
    for a in left:
        for b in right:
            term = dot(a, b, dims)
            total = term if total is None else total + term
    return total


def dot_high(left, right, dims=((1,), (0,))):
    return lax.dot_general(
        left, right, (dims, ((), ())), preferred_element_type=F32, precision=lax.Precision.HIGHEST
    )


def tile_rows(t):
    return pl.ds(pl.multiple_of(t * TILE, TILE), TILE)


def edges(t):
    row = lax.broadcasted_iota(jnp.int32, (TILE, 256), 0).astype(F32) + float(t * TILE)
    line = jnp.floor((row + 0.5) * (1.0 / SIDE))
    column = row - line * SIDE
    image = jnp.floor((line + 0.5) * (1.0 / SIDE))
    return line - image * SIDE, column


def shifted_tiles(padded, columns, sign):
    for t in range(columns.shape[0] // TILE):
        line, column = edges(t)
        at = slice(t * TILE, t * TILE + TILE)
        for tap in range(9):
            dr, dc = sign * (tap // 3 - 1), sign * (tap % 3 - 1)
            start = t * TILE + PAD + dr * SIDE + dc
            value = padded[start : start + TILE, :]
            keep = None
            if dr:
                keep = line > 0.5 if dr < 0 else line < SIDE - 1.5
            if dc:
                side = column > 0.5 if dc < 0 else column < SIDE - 1.5
                keep = side if keep is None else keep & side
            if keep is not None:
                value = jnp.where(keep, value, 0.0)
            columns[at, tap * 256 : tap * 256 + 256] = value.astype(BF16)


def lanes_of(rows, right):
    lane = lax.broadcasted_iota(jnp.int32, (rows, 128), 1)
    return lane, lane - (64 if right else 0), lax.broadcasted_iota(jnp.int32, (rows, 128), 0)


def pack_block(square, at, right, row):
    top, low = square[at : at + 32], square[at + 32 : at + 64]
    lane, rel, i = lanes_of(32, right)
    moved = pltpu.roll(low, 96, 1)
    corner = jnp.where(rel > i, top, jnp.where(rel == i, 0.5 * top, moved))
    value = jnp.where(rel < 32, corner, top)
    upper, lower = value[:16], value[16:]
    if right:
        upper = pltpu.roll(upper, 64, 1)
    else:
        lower = pltpu.roll(lower, 64, 1)
    packed = jnp.where(lane[:16] < 64, upper, lower)
    diagonal = jnp.sum(jnp.where(rel - 32 == i, 0.5 * low, 0.0), axis=0, keepdims=True)
    diagonal = pltpu.roll(diagonal, 96 if right else 32, 1)
    if right:
        row = pltpu.roll(row, 64, 1)
    flat = lane[:1]
    return packed, jnp.where(flat < 64, row, jnp.where(flat < 96, diagonal, 0.0))


def half_block(packed, extra, right):
    lane, rel, i = lanes_of(32, right)
    rolled = pltpu.roll(packed, 64, 1)
    value = jnp.concatenate([rolled, packed] if right else [packed, rolled], axis=0)
    diagonal = pltpu.roll(extra, 32 if right else 96, 1)
    inside = (rel >= 0) & (rel < 64)
    top = jnp.where(inside & ((rel >= 32) | (rel >= i)), value, 0.0)
    low = jnp.where(inside & (rel >= 32) & (rel - 32 < i), pltpu.roll(value, 32, 1), 0.0)
    low = jnp.where(rel - 32 == i, diagonal, low)
    return top, low


def fill_diagonal(target, source):
    zero = jnp.zeros((128, 128), F32)
    for pair in range(8):
        j, at = pair // 2, (pair % 2) * 128
        pieces = []
        for right in (False, True):
            k = 2 * pair + int(right)
            pieces += half_block(source[k, :16, :], source[k, 16:17, :], right)
        half = jnp.concatenate(pieces, axis=0)
        target[j, at : at + 128, at : at + 128] = half + half.T
        target[j, at : at + 128, 128 - at : 256 - at] = zero


def fill_row(target, source):
    lane = lax.broadcasted_iota(jnp.int32, (1, 128), 1)
    for pair in range(8):
        right = pltpu.roll(source[2 * pair + 1, 16:17, :], 64, 1)
        target[0:1, pair * 128 : pair * 128 + 128] = jnp.where(lane < 64, source[2 * pair, 16:17, :], right)


def fill_payload(payload, squares, row):
    for j in range(4):
        square = squares(j)
        for q in range(4):
            k = 4 * j + q
            tile = (q // 2) * 128
            packed, extra = pack_block(
                square[:, tile : tile + 128], q * 64, bool(q % 2), row[:, (k // 2) * 128 : (k // 2) * 128 + 128]
            )
            payload[k, :16, :] = packed
            payload[k, 16:17, :] = extra


def block_of(packed, extra):
    top, low = half_block(packed, extra, False)
    half = jnp.concatenate([top, low], axis=0)[:, :64]
    return half + half.T


def packed_of(square, row):
    wide = jnp.concatenate([square, jnp.zeros((64, 64), F32)], axis=1)
    return pack_block(wide, 0, False, jnp.concatenate([row, jnp.zeros((1, 64), F32)], axis=1))


def outer(left, right):
    first = lax.broadcasted_iota(jnp.int32, (8, 64), 0) == 0
    return dot_high(jnp.where(first, left, 0.0), jnp.broadcast_to(right, (8, 64)), ((0,), (0,)))


def eye(size):
    return lax.broadcasted_iota(jnp.int32, (size, size), 0) == lax.broadcasted_iota(jnp.int32, (size, size), 1)


def solve_white(span, packed, extra, keep):
    mean = extra[:, :64] * (1.0 / span)
    cov = block_of(packed, extra) * (1.0 / span) - outer(mean, mean) + jnp.where(eye(64), epsilon, 0.0)
    trace = trace_of(cov)
    white = newton(cov / trace, 64) / jnp.sqrt(jnp.full((64, 64), trace))
    keep[:64] = cov
    keep[64:128] = white
    keep[128:136] = jnp.broadcast_to(mean, (8, 64))
    return packed_of(white, dot_high(jnp.broadcast_to(mean, (8, 64)), white)[:1])


def solve_slope(span, packed, extra, keep):
    cov, white, mean = keep[:64], keep[64:128], keep[128:129]
    csum = extra[:, :64]
    lifted = outer(mean, csum)
    cross = block_of(packed, extra) - 0.5 * (lifted + lifted.T)
    trace = trace_of(cov)
    scaled = cov / trace
    up = jnp.concatenate([scaled, cross / jnp.sqrt(jnp.full((64, 64), trace))], axis=1)
    low = jnp.concatenate([jnp.zeros((64, 64), F32), scaled], axis=1)
    dn = newton(jnp.concatenate([up, low], axis=0), 128)[:64, 64:]
    dt = -jnp.sum(dn * scaled) / trace - 0.5 * jnp.sum(cross * white) / trace
    dcov = dn / trace + jnp.where(eye(64), dt, 0.0)
    sym = dcov + dcov.T
    wide = jnp.broadcast_to(csum, (8, 64))
    line = dot_high(wide, white, ((1,), (1,))) + dot_high(jnp.broadcast_to(mean, (8, 64)), sym)
    return packed_of(sym, line[:1] * (1.0 / span))


def remote(source, target, sems, at, peer):
    send, recv = sems
    return pltpu.make_async_remote_copy(
        src_ref=source, dst_ref=target, send_sem=send.at[at], recv_sem=recv.at[at], device_id=peer,
        device_id_type=MESH,
    )


class Place:
    def __init__(self):
        self.z, ghost = lax.axis_index("group"), lax.axis_index("ghost")
        self.x, self.y, self.core, self.chip = ghost // 8, (ghost // 2) % 4, ghost % 2, ghost // 2

    def chip_peer(self, chip):
        return (self.z, chip * 2 + self.core)

    def partner(self):
        return (self.z, self.chip * 2 + 1 - self.core)

    def along_x(self, s):
        return (self.z, ((self.x + s + 4) % 4) * 8 + self.y * 2 + self.core)

    def along_y(self, s):
        return (self.z, self.x * 8 + ((self.y + s + 4) % 4) * 2 + self.core)

    def along_z(self, s):
        return ((self.z + s) % 8, self.chip * 2 + self.core)

    def greet(self):
        barrier = pltpu.get_barrier_semaphore()

        def signal(peer):
            pl.semaphore_signal(barrier, inc=1, device_id=peer, device_id_type=MESH)

        for s in range(1, 16):
            signal(self.chip_peer((self.chip + s) % 16))
        for s in range(1, 8):
            signal(self.along_z(s))
        signal(self.partner())

    def greeted(self):
        pl.semaphore_wait(pltpu.get_barrier_semaphore(), 23)


def exchange(place, solve, payload, keep, out, got, mine, sems, cover, alone):
    if alone:
        cover()
        for k in range(16):
            value, extra = solve(payload[k, :16, :], payload[k, 16:17, :], keep.at[k])
            out[k, :16, :] = value
            out[k, 16:17, :] = extra
        return
    chip = place.chip
    scatter, spread, swap_sems = sems[0:2], sems[2:4], sems[4:6]

    def outward(s):
        target = (chip + s) % 16
        return remote(payload.at[target], got.at[s], scatter, s, place.chip_peer(target))

    def start(s, carry):
        outward(s).start()
        return carry

    lax.fori_loop(1, 16, start, 0)
    cover()
    mine[0] = payload[chip]

    def add(s, carry):
        outward(s).wait_recv()
        mine[0] += got[s]
        return carry

    lax.fori_loop(1, 16, add, 0)
    swap = remote(mine.at[0], mine.at[1], swap_sems, 0, place.partner())
    swap.start()
    swap.wait_recv()
    value, extra = solve(mine[0, :16, :] + mine[1, :16, :], mine[0, 16:17, :] + mine[1, 16:17, :], keep.at[0])
    mine[2, :16, :] = value
    mine[2, 16:17, :] = extra

    def back(s):
        return remote(mine.at[2], out.at[chip], spread, s, place.chip_peer((chip + s) % 16))

    def arrival(s):
        return remote(mine.at[2], out.at[(chip + 16 - s) % 16], spread, s, place.chip_peer((chip + s) % 16))

    def start_back(s, carry):
        back(s).start()
        return carry

    lax.fori_loop(1, 16, start_back, 0)
    out[chip] = mine[2]

    def finish(s, carry):
        arrival(s).wait_recv()
        return carry

    lax.fori_loop(1, 16, finish, 0)

    def drain(s, carry):
        outward(s).wait_send()
        back(s).wait_send()
        return carry

    lax.fori_loop(1, 16, drain, 0)
    swap.wait_send()


class AxisSum:
    def __init__(self, chunk, me, peer, box, sems, at):
        self.chunk, self.me, self.box = chunk, me, box
        relay, raw, comb, held = (box.at[n] for n in range(4))
        self.held, self.relay_in, self.raw_in, self.comb_in = held, relay, raw, comb
        self.relay, self.raw, self.comb = [], [], []
        for i, s in enumerate((1, -1)):
            to = peer(s)
            near = (me + s + 4) % 4
            self.relay.append(remote(chunk((me + 2) % 4, i), relay.at[i], sems, at + 3 * i, to))
            self.raw.append(remote(chunk(near, 1 - i), raw.at[i], sems, at + 3 * i + 1, to))
            self.comb.append(remote(held.at[i], comb.at[i], sems, at + 3 * i + 2, to))

    def begin(self):
        for i in range(2):
            self.relay[i].start()
        for i in range(2):
            self.raw[i].start()

    def combine(self):
        for i, s in enumerate((1, -1)):
            near = (self.me + s + 4) % 4
            self.relay[i].wait_recv()
            for n in range(2):
                self.held[i, n] = self.chunk(near, i)[n] + self.relay_in[i, n]
            self.comb[i].start()

    def end(self, store):
        for i in range(2):
            self.comb[i].wait_recv()
            self.raw[1 - i].wait_recv()
            for n in range(2):
                store(2 * i + n, self.chunk(self.me, i)[n] + self.comb_in[i, n] + self.raw_in[1 - i, n])

    def drain(self):
        for one in self.relay + self.raw + self.comb:
            one.wait_send()


class OwnerSum:
    def __init__(self, place, grads, other, total, half, last, wide, thin, sems):
        self.place, self.grads, self.other, self.total = place, grads, other, total
        self.half, self.last = half, last
        core = place.core
        self.swaps = [
            remote(grads.at[1 - core, 4 * h : 4 * h + 4], other.at[4 * h : 4 * h + 4], sems, h, place.partner())
            for h in range(2)
        ]
        self.wide = [
            AxisSum(lambda d, n: total.at[2 * n : 2 * n + 2, d], place.x, place.along_x, wide.at[0], sems, 2),
            AxisSum(lambda d, n: total.at[4 + 2 * n : 6 + 2 * n, :, d], place.y, place.along_y, wide.at[1], sems, 8),
        ]
        self.thin = [
            AxisSum(lambda d, n: half.at[0, 2 * n : 2 * n + 2, d], place.y, place.along_y, thin.at[0], sems, 14),
            AxisSum(lambda d, n: half.at[1, 2 * n : 2 * n + 2, d], place.x, place.along_x, thin.at[1], sems, 20),
        ]
        self.final = [
            remote(last.at[0, (place.z + s) % 8], last.at[1, s], sems, 25 + s, place.along_z(s)) for s in range(1, 8)
        ]

    def swap(self):
        for one in self.swaps:
            one.start()

    def join(self):
        for h in range(2):
            self.swaps[h].wait_recv()

            def body(i, carry):
                self.total[4 * h + i] = self.grads[self.place.core, 4 * h + i] + self.other[4 * h + i]
                return carry

            lax.fori_loop(0, 4, body, 0)
            self.wide[h].begin()

    def combine_wide(self):
        for h in range(2):
            self.wide[h].combine()

    def turn(self):
        for h in range(2):

            def store(n, value):
                self.half[h, n] = value

            self.wide[h].end(store)
            self.thin[h].begin()

    def combine_thin(self):
        for h in range(2):
            self.thin[h].combine()

    def deepen(self):
        for h in range(2):

            def store(n, value):
                self.last[0, 4 * h + n] = value

            self.thin[h].end(store)
        for one in self.final:
            one.start()

    def result(self):
        value = self.last[0, self.place.z]
        for s in range(1, 8):
            self.final[s - 1].wait_recv()
            value = value + self.last[1, s]
        return value

    def drain(self):
        for one in self.swaps + self.final:
            one.wait_send()
        for one in self.wide + self.thin:
            one.drain()


EARLY, LATE = 32, 8


def slot_rows(core, slot, slots):
    return pl.ds(core * 128 * slots + slot, 128, stride=slots)


def pack_gains(gains):
    total = jnp.sum(gains[...], axis=0, keepdims=True)
    row = lax.broadcasted_iota(jnp.int32, (256, 1024), 0)
    own = (row & 127) * 2 + (row >> 7)
    channel = lax.broadcasted_iota(jnp.int32, (256, 1024), 1)
    spread = jnp.where((channel >> 2) == own, total, 0.0)
    channel = lax.broadcasted_iota(jnp.int32, (1024, 128), 0)
    lane = lax.broadcasted_iota(jnp.int32, (1024, 128), 1)
    pick = jnp.where((channel & 3) == lane, 1.0, 0.0).astype(BF16)
    return dot_parts(parts(spread, 3), [pick])


def kernel(
    span, scale, alone,
    x_in, og_in, a_in, b_in, c_in, gain, input_grad, sums, *scratch,
):
    (
        x, og, a, b, c, acc, padded, columns, h1, s1, h2, s2, gram, hsum, wide, payload, payload2, keep, whites,
        slopes, got, got2, mine, mine2, diagonal, diagonal2, row, white, dpre, dwhite, d, across, csum, gains, e,
        last, mid, top, early, late, early_other, late_other, early_total, late_total, early_half, late_half,
        early_last, late_last, early_wide, late_wide, early_thin, late_thin, grad_out, load_sems, *sems,
    ) = scratch
    place = None if alone else Place()
    loads = [
        pltpu.make_async_copy(source, target, load_sems.at[n])
        for n, (source, target) in enumerate(((a_in, a), (x_in, x), (b_in, b), (c_in, c), (og_in, og)))
    ]
    for one in loads:
        one.start()
    if not alone:
        place.greet()
    rows = x.shape[0]
    padded[:PAD, :] = jnp.zeros((PAD, 256), F32)
    padded[rows + PAD :, :] = jnp.zeros((PAD, 256), F32)

    loads[0].wait()
    loads[1].wait()
    acc[...] = dot(x[...], a[...])

    def first(t, carry):
        v = acc[tile_rows(t), :]
        s = 1.0 / (1.0 + jnp.exp(-v))
        s1[tile_rows(t), :] = s * (1.0 + v * (1.0 - s))
        h = (v * s).astype(BF16)
        h1[tile_rows(t), :] = h
        padded[pl.ds(t * TILE + PAD, TILE), :] = h.astype(F32)
        return carry

    lax.fori_loop(0, rows // TILE, first, 0)
    shifted_tiles(padded, columns, 1)
    loads[2].wait()
    acc[...] = dot(columns[...], b[...])

    def second(t, carry):
        v = acc[tile_rows(t), :]
        s = 1.0 / (1.0 + jnp.exp(-v))
        s2[tile_rows(t), :] = s * (1.0 + v * (1.0 - s))
        h2[tile_rows(t), :] = (v * s).astype(BF16)
        return carry

    lax.fori_loop(0, rows // TILE, second, 0)
    gram[...] = dot(h2[...], h2[...], ((0,), (0,)))
    loads[3].wait()
    wide[...] = dot_parts(parts(gram[...], 3), [c[...]])
    brow = dot_parts(parts(dot(jnp.ones((8, rows), BF16), h2[...]), 3), [c[...]])

    def squares(j):
        here = slice(j * 256, j * 256 + 256)
        return dot_parts([c[:, here]], parts(wide[:, here], 3), ((0,), (0,)))

    fill_payload(payload, squares, brow[:1])
    if not alone:
        place.greeted()

    def cover():
        hsum[...] = dot(h2[...], jnp.ones((rows, 128), BF16), ((0,), (0,)))
        loads[4].wait()

    exchange(
        place, lambda *args: solve_white(span, *args), payload, keep, whites, got, mine, sems[0:6], cover, alone
    )

    fill_diagonal(diagonal, whites)
    fill_row(row, whites)
    for j in range(4):
        here = slice(j * 256, j * 256 + 256)
        folded = dot_parts([c[:, here]], parts(diagonal[j], 2))
        high, low = parts(folded, 2)
        d[:, here] = high
        white[:, here] = dot(h2[...], high) + dot(h2[...], low)
    csum[...] = jnp.zeros_like(csum)
    gains[...] = jnp.zeros_like(gains)

    def slope(t, carry):
        for j in range(8):
            here = slice(j * 128, j * 128 + 128)
            w = white[tile_rows(t), here] - row[0:1, here]
            g = gain[0:1, here]
            v = x[tile_rows(t), here].astype(F32) + g * w
            s = 1.0 / (1.0 + jnp.exp(-v))
            u = og[tile_rows(t), here].astype(F32) * (s * (1.0 + v * (1.0 - s)))
            dpre[tile_rows(t), here] = u
            dw = g * u
            dwhite[tile_rows(t), here] = dw.astype(BF16)
            csum[:, here] += jnp.sum(dw.reshape(TILE // 8, 8, 128), axis=0)
            gains[:, here] += jnp.sum((u * w).reshape(TILE // 8, 8, 128), axis=0)
        return carry

    lax.fori_loop(0, rows // TILE, slope, 0)
    across[...] = dot(h2[...], dwhite[...], ((0,), (0,)))

    def squares2(j):
        here = slice(j * 256, j * 256 + 256)
        square = dot_parts([c[:, here]], parts(across[:, here], 2), ((0,), (0,)))
        return 0.5 * (square + square.T)

    fill_payload(payload2, squares2, jnp.sum(csum[...], axis=0, keepdims=True))

    def cover2():
        acc[...] = dot(dwhite[...], d[...], ((1,), (1,)))
        for j in range(4):
            here = slice(j * 256, j * 256 + 256)
            high, low = parts(across[:, here], 2)
            pieces = parts(diagonal[j], 2)
            value = dot_parts([high], pieces, ((1,), (1,))) + dot(low, pieces[0], ((1,), (1,)))
            for half in range(2):
                last[2 * j + half] = value[:, half * 128 : half * 128 + 128]

    exchange(
        place, lambda *args: solve_slope(span, *args), payload2, keep, slopes, got2, mine2, sems[6:12], cover2, alone
    )

    fill_diagonal(diagonal2, slopes)
    fill_row(row, slopes)
    for j in range(4):
        here = slice(j * 256, j * 256 + 256)
        e[:, here] = (dot_parts([c[:, here]], parts(diagonal2[j], 2)) * (1.0 / span)).astype(BF16)
    back = dot(e[...], c[...], ((1,), (1,))).astype(BF16)
    const = dot_parts(parts(jnp.broadcast_to(row[0:1, :], (8, 1024)), 2), [c[...]], ((1,), (1,)))
    acc[...] += dot(h2[...], back)

    def dmid2(t, carry):
        v = (acc[tile_rows(t), :] - const[0:1, :]) * s2[tile_rows(t), :]
        padded[pl.ds(t * TILE + PAD, TILE), :] = v.astype(BF16).astype(F32)
        return carry

    lax.fori_loop(0, rows // TILE, dmid2, 0)
    shifted_tiles(padded, columns, -1)
    for tap in range(9):
        here = slice(tap * 256, tap * 256 + 256)
        value = dot(h1[...], columns[:, here], ((0,), (0,)))
        for half in range(2):
            mid[half, here, :] = value[:, half * 128 : half * 128 + 128]
    grams = parts(gram[...], 2)
    for j in range(4):
        value = dot_parts(grams, [e[:, j * 256 : j * 256 + 256]])
        for half in range(2):
            n = 2 * j + half
            here = slice(n * 128, n * 128 + 128)
            last[n] = last[n] + value[:, half * 128 : half * 128 + 128] - hsum[...] * row[0:1, here]
    value = pack_gains(gains)
    for core in range(2):
        for j in range(8):
            early[slot_rows(core, j, EARLY), :] = last[j, pl.ds(core, 128, stride=2), :]
        for half in range(2):
            for q in range(9):
                early[slot_rows(core, 8 + 2 * q + half, EARLY), :] = mid[half, pl.ds(q + 9 * core, 128, stride=18), :]
        early[slot_rows(core, 26, EARLY), :] = value[core * 128 : core * 128 + 128]
        for slot in range(27, 32):
            early[slot_rows(core, slot, EARLY), :] = jnp.zeros((128, 128), F32)
    if not alone:
        early_sum = OwnerSum(
            place, early.reshape(2, 8, 4, 4, EARLY, 128), early_other, early_total, early_half, early_last,
            early_wide, early_thin, sems[12:14],
        )
        late_sum = OwnerSum(
            place, late.reshape(2, 8, 4, 4, LATE, 128), late_other, late_total, late_half, late_last, late_wide,
            late_thin, sems[14:16],
        )
        early_sum.swap()
    for tap in range(9):
        here = slice(tap * 256, tap * 256 + 256)
        term = dot(columns[:, here], b[here, :], ((1,), (1,)))
        if tap == 0:
            acc[...] = term
        else:
            acc[...] += term
    if not alone:
        early_sum.join()

    def dmid1(t, carry):
        dwhite[tile_rows(t), :256] = (acc[tile_rows(t), :] * s1[tile_rows(t), :]).astype(BF16)
        return carry

    lax.fori_loop(0, rows // TILE, dmid1, 0)
    value = dot(x[...], dwhite[:, :256], ((0,), (0,)))
    for half in range(2):
        top[half] = value[:, half * 128 : half * 128 + 128]
    for core in range(2):
        for half in range(2):
            for q in range(4):
                late[slot_rows(core, 2 * q + half, LATE), :] = top[half, pl.ds(q + 4 * core, 128, stride=8), :]
    if not alone:
        late_sum.swap()
        early_sum.combine_wide()
    for j in range(4):
        here = slice(j * 256, j * 256 + 256)
        grad_out[:, here] = (dot(dwhite[:, :256], a[here, :], ((1,), (1,))) + dpre[:, here]).astype(BF16)
    store = pltpu.make_async_copy(grad_out, input_grad, load_sems.at[5])
    store.start()
    if alone:
        sums[:, :32, :] = early[...].reshape(256, 32, 128)
        sums[:, 32:, :] = late[...].reshape(256, 8, 128)
    else:
        late_sum.join()
        early_sum.turn()
        late_sum.combine_wide()
        early_sum.combine_thin()
        late_sum.turn()
        early_sum.deepen()
        late_sum.combine_thin()
        late_sum.deepen()
        sums[:EARLY, :] = early_sum.result() * scale
        sums[EARLY:, :] = late_sum.result() * scale
        early_sum.drain()
        late_sum.drain()
    store.wait()


VM = pl.BlockSpec(memory_space=pltpu.VMEM)
ANY = pl.BlockSpec(memory_space=pl.ANY)


def shape(dims, kind=F32):
    return jax.ShapeDtypeStruct(dims, kind)


def block_step(inputs, out_grad, conv_first, conv_middle, conv_last, gain, span, scale, alone=False):
    rows = inputs.shape[0]

    def body(*refs):
        kernel(span, scale, alone, *refs)

    def vmem(*dims, kind=F32):
        return pltpu.VMEM(dims, kind)

    dma = pltpu.SemaphoreType.DMA
    grown = [vmem(8, 4, 4, size, 128) for size in (EARLY, LATE)]
    scratch = [
        vmem(rows, 1024, kind=BF16), vmem(rows, 1024, kind=BF16), vmem(1024, 256, kind=BF16),
        vmem(2304, 256, kind=BF16), vmem(256, 1024, kind=BF16),
        vmem(rows, 256), vmem(rows + 2 * PAD, 256), vmem(rows, 2304, kind=BF16),
        vmem(rows, 256, kind=BF16), vmem(rows, 256), vmem(rows, 256, kind=BF16), vmem(rows, 256),
        vmem(256, 256), vmem(256, 128), vmem(256, 1024),
        vmem(16, 17, 128), vmem(16, 17, 128), vmem(16 if alone else 1, 136, 64),
        vmem(16, 17, 128), vmem(16, 17, 128), vmem(16, 17, 128), vmem(16, 17, 128),
        vmem(3, 17, 128), vmem(3, 17, 128),
        vmem(4, 256, 256), vmem(4, 256, 256), vmem(8, 1024),
        vmem(rows, 1024), vmem(rows, 1024), vmem(rows, 1024, kind=BF16), vmem(256, 1024, kind=BF16),
        vmem(256, 1024), vmem(8, 1024), vmem(8, 1024), vmem(256, 1024, kind=BF16),
        vmem(8, 256, 128), vmem(2, 2304, 128), vmem(2, 1024, 128),
        vmem(256 * EARLY, 128), vmem(256 * LATE, 128), *grown, *grown,
        vmem(2, 4, 4, EARLY, 128), vmem(2, 4, 4, LATE, 128),
        vmem(2, 8, EARLY, 128), vmem(2, 8, LATE, 128),
        vmem(2, 4, 2, 2, 4, EARLY, 128), vmem(2, 4, 2, 2, 4, LATE, 128),
        vmem(2, 4, 2, 2, EARLY, 128), vmem(2, 4, 2, 2, LATE, 128),
        vmem(rows, 1024, kind=BF16),
        dma((6,)), *([dma((16,))] * 4 + [dma((1,))] * 2) * 2, *[dma((33,))] * 4,
    ]
    params = {} if alone else dict(collective_id=0, has_side_effects=True)
    return pl.pallas_call(
        body,
        out_shape=(shape((rows, 1024), BF16), shape((256, 40, 128) if alone else (EARLY + LATE, 128))),
        in_specs=[ANY] * 5 + [VM],
        out_specs=(ANY, VM),
        scratch_shapes=scratch,
        compiler_params=pltpu.CompilerParams(vmem_limit_bytes=67043328, **params),
        name="block_step",
    )(inputs, out_grad, conv_first, conv_middle, conv_last, gain.reshape(1, -1))


def shards(inputs, out_grad, conv_first, conv_middle, conv_last, gain):
    ghosts, groups = lax.axis_size("ghost"), lax.axis_size("group")
    span = float(inputs.shape[0] * ghosts)
    input_grad, sums = block_step(
        inputs, out_grad, conv_first, conv_middle, conv_last, gain, span, (span * groups) ** (-0.5)
    )
    return (
        input_grad, sums[32:40].reshape(-1), sums[8:26].reshape(-1), sums[0:8].reshape(-1), sums[26, :4]
    )


def newton(n, size):
    row = lax.broadcasted_iota(jnp.int32, (size, size), 0)
    lane = lax.broadcasted_iota(jnp.int32, (size, size), 1)
    project = jnp.where(row == lane, 1.5, 0.0) - 0.5 * n
    for sweep in range(NEWTON - 1):
        squared = dot_high(project, project)
        project = 1.5 * project - 0.5 * dot_high(squared, dot_high(project, n))
    return project


def trace_of(block, size=64):
    row = lax.broadcasted_iota(jnp.int32, (size, size), 0)
    lane = lax.broadcasted_iota(jnp.int32, (size, size), 1)
    return jnp.sum(jnp.where(row == lane, block, 0.0))


def solution(mesh):
    rows = P(("group", "ghost"))
    return jax.shard_map(
        shards,
        mesh=mesh,
        in_specs=(P(("group", "ghost"), None), P(("group", "ghost"), None), P(), P(), P(), P()),
        out_specs=(P(("group", "ghost"), None), rows, rows, rows, rows),
        check_vma=False,
    )
```

```python
import jax
import jax.numpy as jnp
from jax import lax
from jax.experimental import pallas as pl
from jax.experimental.pallas import tpu as pltpu
from jax.sharding import PartitionSpec as P

GROUP = 64
NEWTON = 5
SIDE = 14
PAD = 16
TILE = 112
MESH = pl.DeviceIdType.MESH
epsilon = 1e-05
F32 = jnp.float32
BF16 = jnp.bfloat16


def dot(left, right, dims=((1,), (0,))):
    return lax.dot_general(left, right, (dims, ((), ())), preferred_element_type=F32)


def parts(value, count):
    pieces = []
    for _ in range(count):
        piece = value.astype(BF16)
        pieces.append(piece)
        value = value - piece.astype(F32)
    return pieces


def dot_parts(left, right, dims=((1,), (0,))):
    total = None
    for a in left:
        for b in right:
            term = dot(a, b, dims)
            total = term if total is None else total + term
    return total


def dot_high(left, right, dims=((1,), (0,))):
    return lax.dot_general(
        left, right, (dims, ((), ())), preferred_element_type=F32, precision=lax.Precision.HIGHEST
    )


def tile_rows(t):
    return pl.ds(pl.multiple_of(t * TILE, TILE), TILE)


def edges(t):
    row = lax.broadcasted_iota(jnp.int32, (TILE, 256), 0).astype(F32) + float(t * TILE)
    line = jnp.floor((row + 0.5) * (1.0 / SIDE))
    column = row - line * SIDE
    image = jnp.floor((line + 0.5) * (1.0 / SIDE))
    return line - image * SIDE, column


def shifted_tiles(padded, columns, sign):
    for t in range(columns.shape[0] // TILE):
        line, column = edges(t)
        at = slice(t * TILE, t * TILE + TILE)
        for tap in range(9):
            dr, dc = sign * (tap // 3 - 1), sign * (tap % 3 - 1)
            start = t * TILE + PAD + dr * SIDE + dc
            value = padded[start : start + TILE, :]
            keep = None
            if dr:
                keep = line > 0.5 if dr < 0 else line < SIDE - 1.5
            if dc:
                side = column > 0.5 if dc < 0 else column < SIDE - 1.5
                keep = side if keep is None else keep & side
            if keep is not None:
                value = jnp.where(keep, value, 0.0)
            columns[at, tap * 256 : tap * 256 + 256] = value.astype(BF16)


def lanes_of(rows, right):
    lane = lax.broadcasted_iota(jnp.int32, (rows, 128), 1)
    return lane, lane - (64 if right else 0), lax.broadcasted_iota(jnp.int32, (rows, 128), 0)


def pack_block(square, at, right, row):
    top, low = square[at : at + 32], square[at + 32 : at + 64]
    lane, rel, i = lanes_of(32, right)
    moved = pltpu.roll(low, 96, 1)
    corner = jnp.where(rel > i, top, jnp.where(rel == i, 0.5 * top, moved))
    value = jnp.where(rel < 32, corner, top)
    upper, lower = value[:16], value[16:]
    if right:
        upper = pltpu.roll(upper, 64, 1)
    else:
        lower = pltpu.roll(lower, 64, 1)
    packed = jnp.where(lane[:16] < 64, upper, lower)
    diagonal = jnp.sum(jnp.where(rel - 32 == i, 0.5 * low, 0.0), axis=0, keepdims=True)
    diagonal = pltpu.roll(diagonal, 96 if right else 32, 1)
    if right:
        row = pltpu.roll(row, 64, 1)
    flat = lane[:1]
    return packed, jnp.where(flat < 64, row, jnp.where(flat < 96, diagonal, 0.0))


def half_block(packed, extra, right):
    lane, rel, i = lanes_of(32, right)
    rolled = pltpu.roll(packed, 64, 1)
    value = jnp.concatenate([rolled, packed] if right else [packed, rolled], axis=0)
    diagonal = pltpu.roll(extra, 32 if right else 96, 1)
    inside = (rel >= 0) & (rel < 64)
    top = jnp.where(inside & ((rel >= 32) | (rel >= i)), value, 0.0)
    low = jnp.where(inside & (rel >= 32) & (rel - 32 < i), pltpu.roll(value, 32, 1), 0.0)
    low = jnp.where(rel - 32 == i, diagonal, low)
    return top, low


def fill_diagonal(target, source):
    zero = jnp.zeros((128, 128), F32)
    for pair in range(8):
        j, at = pair // 2, (pair % 2) * 128
        pieces = []
        for right in (False, True):
            k = 2 * pair + int(right)
            pieces += half_block(source[k, :16, :], source[k, 16:17, :], right)
        half = jnp.concatenate(pieces, axis=0)
        target[j, at : at + 128, at : at + 128] = half + half.T
        target[j, at : at + 128, 128 - at : 256 - at] = zero


def fill_row(target, source):
    lane = lax.broadcasted_iota(jnp.int32, (1, 128), 1)
    for pair in range(8):
        right = pltpu.roll(source[2 * pair + 1, 16:17, :], 64, 1)
        target[0:1, pair * 128 : pair * 128 + 128] = jnp.where(lane < 64, source[2 * pair, 16:17, :], right)


def fill_payload(payload, squares, row):
    for j in range(4):
        square = squares(j)
        for q in range(4):
            k = 4 * j + q
            tile = (q // 2) * 128
            packed, extra = pack_block(
                square[:, tile : tile + 128], q * 64, bool(q % 2), row[:, (k // 2) * 128 : (k // 2) * 128 + 128]
            )
            payload[k, :16, :] = packed
            payload[k, 16:17, :] = extra


def block_of(packed, extra):
    top, low = half_block(packed, extra, False)
    half = jnp.concatenate([top, low], axis=0)[:, :64]
    return half + half.T


def packed_of(square, row):
    wide = jnp.concatenate([square, jnp.zeros((64, 64), F32)], axis=1)
    return pack_block(wide, 0, False, jnp.concatenate([row, jnp.zeros((1, 64), F32)], axis=1))


def outer(left, right):
    first = lax.broadcasted_iota(jnp.int32, (8, 64), 0) == 0
    return dot_high(jnp.where(first, left, 0.0), jnp.broadcast_to(right, (8, 64)), ((0,), (0,)))


def eye(size):
    return lax.broadcasted_iota(jnp.int32, (size, size), 0) == lax.broadcasted_iota(jnp.int32, (size, size), 1)


def solve_white(span, packed, extra, keep):
    mean = extra[:, :64] * (1.0 / span)
    cov = block_of(packed, extra) * (1.0 / span) - outer(mean, mean) + jnp.where(eye(64), epsilon, 0.0)
    trace = trace_of(cov)
    white = newton(cov / trace, 64) / jnp.sqrt(jnp.full((64, 64), trace))
    keep[:64] = cov
    keep[64:128] = white
    keep[128:136] = jnp.broadcast_to(mean, (8, 64))
    return packed_of(white, dot_high(jnp.broadcast_to(mean, (8, 64)), white)[:1])


def solve_slope(span, packed, extra, keep):
    cov, white, mean = keep[:64], keep[64:128], keep[128:129]
    csum = extra[:, :64]
    lifted = outer(mean, csum)
    cross = block_of(packed, extra) - 0.5 * (lifted + lifted.T)
    trace = trace_of(cov)
    scaled = cov / trace
    up = jnp.concatenate([scaled, cross / jnp.sqrt(jnp.full((64, 64), trace))], axis=1)
    low = jnp.concatenate([jnp.zeros((64, 64), F32), scaled], axis=1)
    dn = newton(jnp.concatenate([up, low], axis=0), 128)[:64, 64:]
    dt = -jnp.sum(dn * scaled) / trace - 0.5 * jnp.sum(cross * white) / trace
    dcov = dn / trace + jnp.where(eye(64), dt, 0.0)
    sym = dcov + dcov.T
    wide = jnp.broadcast_to(csum, (8, 64))
    line = dot_high(wide, white, ((1,), (1,))) + dot_high(jnp.broadcast_to(mean, (8, 64)), sym)
    return packed_of(sym, line[:1] * (1.0 / span))


def newton(n, size):
    row = lax.broadcasted_iota(jnp.int32, (size, size), 0)
    lane = lax.broadcasted_iota(jnp.int32, (size, size), 1)
    project = jnp.where(row == lane, 1.5, 0.0) - 0.5 * n
    for sweep in range(NEWTON - 1):
        squared = dot_high(project, project)
        project = 1.5 * project - 0.5 * dot_high(squared, dot_high(project, n))
    return project


def trace_of(block, size=64):
    row = lax.broadcasted_iota(jnp.int32, (size, size), 0)
    lane = lax.broadcasted_iota(jnp.int32, (size, size), 1)
    return jnp.sum(jnp.where(row == lane, block, 0.0))


def remote(source, target, sems, at, peer):
    send, recv = sems
    return pltpu.make_async_remote_copy(
        src_ref=source, dst_ref=target, send_sem=send.at[at], recv_sem=recv.at[at], device_id=peer,
        device_id_type=MESH,
    )


class Place:
    def __init__(self):
        self.z, ghost = lax.axis_index("group"), lax.axis_index("ghost")
        self.x, self.y, self.core, self.chip = ghost // 8, (ghost // 2) % 4, ghost % 2, ghost // 2

    def chip_peer(self, chip):
        return (self.z, chip * 2 + self.core)

    def partner(self):
        return (self.z, self.chip * 2 + 1 - self.core)

    def along_x(self, s):
        return (self.z, ((self.x + s + 4) % 4) * 8 + self.y * 2 + self.core)

    def along_y(self, s):
        return (self.z, self.x * 8 + ((self.y + s + 4) % 4) * 2 + self.core)

    def along_z(self, s):
        return ((self.z + s) % 8, self.chip * 2 + self.core)

    def greet(self):
        barrier = pltpu.get_barrier_semaphore()

        def signal(peer):
            pl.semaphore_signal(barrier, inc=1, device_id=peer, device_id_type=MESH)

        for s in range(1, 16):
            signal(self.chip_peer((self.chip + s) % 16))
        for s in range(1, 8):
            signal(self.along_z(s))
        signal(self.partner())

    def greeted(self):
        pl.semaphore_wait(pltpu.get_barrier_semaphore(), 23)


def exchange(place, solve, payload, keep, out, got, mine, sems, cover, alone):
    if alone:
        cover()
        for k in range(16):
            value, extra = solve(payload[k, :16, :], payload[k, 16:17, :], keep.at[k])
            out[k, :16, :] = value
            out[k, 16:17, :] = extra
        return
    chip = place.chip
    scatter, spread, swap_sems = sems[0:2], sems[2:4], sems[4:6]

    def outward(s):
        target = (chip + s) % 16
        return remote(payload.at[target], got.at[s], scatter, s, place.chip_peer(target))

    def start(s, carry):
        outward(s).start()
        return carry

    lax.fori_loop(1, 16, start, 0)
    cover()
    mine[0] = payload[chip]

    def add(s, carry):
        outward(s).wait_recv()
        mine[0] += got[s]
        return carry

    lax.fori_loop(1, 16, add, 0)
    swap = remote(mine.at[0], mine.at[1], swap_sems, 0, place.partner())
    swap.start()
    swap.wait_recv()
    value, extra = solve(mine[0, :16, :] + mine[1, :16, :], mine[0, 16:17, :] + mine[1, 16:17, :], keep.at[0])
    mine[2, :16, :] = value
    mine[2, 16:17, :] = extra

    def back(s):
        return remote(mine.at[2], out.at[chip], spread, s, place.chip_peer((chip + s) % 16))

    def arrival(s):
        return remote(mine.at[2], out.at[(chip + 16 - s) % 16], spread, s, place.chip_peer((chip + s) % 16))

    def start_back(s, carry):
        back(s).start()
        return carry

    lax.fori_loop(1, 16, start_back, 0)
    out[chip] = mine[2]

    def finish(s, carry):
        arrival(s).wait_recv()
        return carry

    lax.fori_loop(1, 16, finish, 0)

    def drain(s, carry):
        outward(s).wait_send()
        back(s).wait_send()
        return carry

    lax.fori_loop(1, 16, drain, 0)
    swap.wait_send()


class AxisSum:
    def __init__(self, chunk, me, peer, box, sems, at):
        self.chunk, self.me, self.box = chunk, me, box
        relay, raw, comb, held = (box.at[n] for n in range(4))
        self.held, self.relay_in, self.raw_in, self.comb_in = held, relay, raw, comb
        self.relay, self.raw, self.comb = [], [], []
        for i, s in enumerate((1, -1)):
            to = peer(s)
            near = (me + s + 4) % 4
            self.relay.append(remote(chunk((me + 2) % 4, i), relay.at[i], sems, at + 3 * i, to))
            self.raw.append(remote(chunk(near, 1 - i), raw.at[i], sems, at + 3 * i + 1, to))
            self.comb.append(remote(held.at[i], comb.at[i], sems, at + 3 * i + 2, to))

    def begin(self):
        for i in range(2):
            self.relay[i].start()
        for i in range(2):
            self.raw[i].start()

    def combine(self):
        for i, s in enumerate((1, -1)):
            near = (self.me + s + 4) % 4
            self.relay[i].wait_recv()
            for n in range(2):
                self.held[i, n] = self.chunk(near, i)[n] + self.relay_in[i, n]
            self.comb[i].start()

    def end(self, store):
        for i in range(2):
            self.comb[i].wait_recv()
            self.raw[1 - i].wait_recv()
            for n in range(2):
                store(2 * i + n, self.chunk(self.me, i)[n] + self.comb_in[i, n] + self.raw_in[1 - i, n])

    def drain(self):
        for one in self.relay + self.raw + self.comb:
            one.wait_send()


class OwnerSum:
    def __init__(self, place, grads, other, total, half, last, wide, thin, *sems):
        self.place, self.other, self.total = place, other, total
        self.half, self.last = half, last
        used, slots = other.shape[3], grads.shape[0] // 256
        grads = grads.reshape(2, 8, 4, 4, slots, 128)
        self.own = lambda z: grads[place.core, z, :, :, :used, :]
        self.swaps = [
            remote(
                grads.at[1 - place.core, 4 * h : 4 * h + 4, :, :, :used, :], other.at[4 * h : 4 * h + 4], sems, h,
                place.partner(),
            )
            for h in range(2)
        ]
        self.wide = [
            AxisSum(lambda d, n: total.at[2 * n : 2 * n + 2, d], place.x, place.along_x, wide.at[0], sems, 2),
            AxisSum(lambda d, n: total.at[4 + 2 * n : 6 + 2 * n, :, d], place.y, place.along_y, wide.at[1], sems, 8),
        ]
        self.thin = [
            AxisSum(lambda d, n: half.at[0, 2 * n : 2 * n + 2, d], place.y, place.along_y, thin.at[0], sems, 14),
            AxisSum(lambda d, n: half.at[1, 2 * n : 2 * n + 2, d], place.x, place.along_x, thin.at[1], sems, 20),
        ]
        self.final = [
            remote(last.at[0, (place.z + s) % 8], last.at[1, s], sems, 25 + s, place.along_z(s)) for s in range(1, 8)
        ]

    def swap(self):
        for one in self.swaps:
            one.start()

    def join(self):
        for h in range(2):
            self.swaps[h].wait_recv()

            def body(i, carry):
                self.total[4 * h + i] = self.own(4 * h + i) + self.other[4 * h + i]
                return carry

            lax.fori_loop(0, 4, body, 0)
            self.wide[h].begin()

    def combine_wide(self):
        for h in range(2):
            self.wide[h].combine()

    def turn(self):
        for h in range(2):

            def store(n, value):
                self.half[h, n] = value

            self.wide[h].end(store)
            self.thin[h].begin()

    def combine_thin(self):
        for h in range(2):
            self.thin[h].combine()

    def deepen(self):
        for h in range(2):

            def store(n, value):
                self.last[0, 4 * h + n] = value

            self.thin[h].end(store)
        for one in self.final:
            one.start()

    def result(self):
        value = self.last[0, self.place.z]
        for s in range(1, 8):
            self.final[s - 1].wait_recv()
            value = value + self.last[1, s]
        return value

    def drain(self):
        for one in self.swaps + self.final:
            one.wait_send()
        for one in self.wide + self.thin:
            one.drain()


def slot_rows(core, slot, slots):
    return pl.ds(core * 128 * slots + slot, 128, stride=slots)


USED = (8, 19, 8)
SLOTS = (8, 24, 8)


def store_slots(target, source, count, step, at):
    slots = target.shape[0] // 256
    for core in range(2):
        for n in range(source.shape[0]):
            for q in range(count):
                rows = pl.ds(q + step * core, 128, stride=2 * step)
                target[slot_rows(core, at + n + q * source.shape[0], slots), :] = source[n, rows, :]


def pack_gains(gains):
    total = jnp.sum(gains[...], axis=0, keepdims=True)
    row = lax.broadcasted_iota(jnp.int32, (256, 1024), 0)
    own = (row & 127) * 2 + (row >> 7)
    channel = lax.broadcasted_iota(jnp.int32, (256, 1024), 1)
    spread = jnp.where((channel >> 2) == own, total, 0.0)
    channel = lax.broadcasted_iota(jnp.int32, (1024, 128), 0)
    lane = lax.broadcasted_iota(jnp.int32, (1024, 128), 1)
    pick = jnp.where((channel & 3) == lane, 1.0, 0.0).astype(BF16)
    return dot_parts(parts(spread, 3), [pick])


def kernel(
    span, scale, alone,
    x_in, og_in, a_in, b_in, c_in, gain, input_grad, sums, *scratch,
):
    (
        x, og, a, b, c, acc, padded, columns, h1, s1, h2, s2, gram, hsum, wide, payload, payload2, keep, whites,
        slopes, got, got2, mine, mine2, diagonal, diagonal2, row, white, dpre, dwhite, d, across, csum, gains, e,
        last, mid, top, grad_out, load_sems, *rest,
    ) = scratch
    sems, rest = rest[:12], rest[12:]
    groups = [rest[n :: 3] for n in range(3)]
    place = None if alone else Place()
    loads = [
        pltpu.make_async_copy(source, target, load_sems.at[n])
        for n, (source, target) in enumerate(((a_in, a), (x_in, x), (b_in, b), (c_in, c), (og_in, og)))
    ]
    for one in loads:
        one.start()
    if not alone:
        place.greet()
    rows = x.shape[0]
    padded[:PAD, :] = jnp.zeros((PAD, 256), F32)
    padded[rows + PAD :, :] = jnp.zeros((PAD, 256), F32)

    loads[0].wait()
    loads[1].wait()
    acc[...] = dot(x[...], a[...])

    def first(t, carry):
        v = acc[tile_rows(t), :]
        s = 1.0 / (1.0 + jnp.exp(-v))
        s1[tile_rows(t), :] = s * (1.0 + v * (1.0 - s))
        h = (v * s).astype(BF16)
        h1[tile_rows(t), :] = h
        padded[pl.ds(t * TILE + PAD, TILE), :] = h.astype(F32)
        return carry

    lax.fori_loop(0, rows // TILE, first, 0)
    shifted_tiles(padded, columns, 1)
    loads[2].wait()
    acc[...] = dot(columns[...], b[...])

    def second(t, carry):
        v = acc[tile_rows(t), :]
        s = 1.0 / (1.0 + jnp.exp(-v))
        s2[tile_rows(t), :] = s * (1.0 + v * (1.0 - s))
        h2[tile_rows(t), :] = (v * s).astype(BF16)
        return carry

    lax.fori_loop(0, rows // TILE, second, 0)
    gram[...] = dot(h2[...], h2[...], ((0,), (0,)))
    loads[3].wait()
    wide[...] = dot_parts(parts(gram[...], 3), [c[...]])
    brow = dot_parts(parts(dot(jnp.ones((8, rows), BF16), h2[...]), 3), [c[...]])

    def squares(j):
        here = slice(j * 256, j * 256 + 256)
        return dot_parts([c[:, here]], parts(wide[:, here], 3), ((0,), (0,)))

    fill_payload(payload, squares, brow[:1])
    if not alone:
        place.greeted()

    def cover():
        hsum[...] = dot(h2[...], jnp.ones((rows, 128), BF16), ((0,), (0,)))
        loads[4].wait()

    exchange(
        place, lambda *args: solve_white(span, *args), payload, keep, whites, got, mine, sems[0:6], cover, alone
    )

    fill_diagonal(diagonal, whites)
    fill_row(row, whites)
    for j in range(4):
        here = slice(j * 256, j * 256 + 256)
        folded = dot_parts([c[:, here]], parts(diagonal[j], 2))
        high, low = parts(folded, 2)
        d[:, here] = high
        white[:, here] = dot(h2[...], high) + dot(h2[...], low)
    csum[...] = jnp.zeros_like(csum)
    gains[...] = jnp.zeros_like(gains)

    def slope(t, carry):
        for j in range(8):
            here = slice(j * 128, j * 128 + 128)
            w = white[tile_rows(t), here] - row[0:1, here]
            g = gain[0:1, here]
            v = x[tile_rows(t), here].astype(F32) + g * w
            s = 1.0 / (1.0 + jnp.exp(-v))
            u = og[tile_rows(t), here].astype(F32) * (s * (1.0 + v * (1.0 - s)))
            dpre[tile_rows(t), here] = u
            dw = g * u
            dwhite[tile_rows(t), here] = dw.astype(BF16)
            csum[:, here] += jnp.sum(dw.reshape(TILE // 8, 8, 128), axis=0)
            gains[:, here] += jnp.sum((u * w).reshape(TILE // 8, 8, 128), axis=0)
        return carry

    lax.fori_loop(0, rows // TILE, slope, 0)
    across[...] = dot(h2[...], dwhite[...], ((0,), (0,)))

    def squares2(j):
        here = slice(j * 256, j * 256 + 256)
        square = dot_parts([c[:, here]], parts(across[:, here], 2), ((0,), (0,)))
        return 0.5 * (square + square.T)

    fill_payload(payload2, squares2, jnp.sum(csum[...], axis=0, keepdims=True))

    def cover2():
        acc[...] = dot(dwhite[...], d[...], ((1,), (1,)))
        for j in range(4):
            here = slice(j * 256, j * 256 + 256)
            high, low = parts(across[:, here], 2)
            pieces = parts(diagonal[j], 2)
            value = dot_parts([high], pieces, ((1,), (1,))) + dot(low, pieces[0], ((1,), (1,)))
            for half in range(2):
                last[2 * j + half] = value[:, half * 128 : half * 128 + 128]

    exchange(
        place, lambda *args: solve_slope(span, *args), payload2, keep, slopes, got2, mine2, sems[6:12], cover2, alone
    )

    fill_diagonal(diagonal2, slopes)
    fill_row(row, slopes)
    for j in range(4):
        here = slice(j * 256, j * 256 + 256)
        e[:, here] = (dot_parts([c[:, here]], parts(diagonal2[j], 2)) * (1.0 / span)).astype(BF16)
    grams = parts(gram[...], 2)
    for j in range(4):
        value = dot_parts(grams, [e[:, j * 256 : j * 256 + 256]])
        for half in range(2):
            n = 2 * j + half
            here = slice(n * 128, n * 128 + 128)
            last[n] = last[n] + value[:, half * 128 : half * 128 + 128] - hsum[...] * row[0:1, here]
    store_slots(groups[0][0], last, 1, 1, 0)
    if alone:
        one = two = three = None
    else:
        one, two, three = (OwnerSum(place, *group) for group in groups)
        one.swap()
    back = dot(e[...], c[...], ((1,), (1,))).astype(BF16)
    const = dot_parts(parts(jnp.broadcast_to(row[0:1, :], (8, 1024)), 2), [c[...]], ((1,), (1,)))
    acc[...] += dot(h2[...], back)

    def dmid2(t, carry):
        v = (acc[tile_rows(t), :] - const[0:1, :]) * s2[tile_rows(t), :]
        padded[pl.ds(t * TILE + PAD, TILE), :] = v.astype(BF16).astype(F32)
        return carry

    lax.fori_loop(0, rows // TILE, dmid2, 0)
    if not alone:
        one.join()
    shifted_tiles(padded, columns, -1)
    if not alone:
        one.combine_wide()
    for tap in range(9):
        here = slice(tap * 256, tap * 256 + 256)
        value = dot(h1[...], columns[:, here], ((0,), (0,)))
        for half in range(2):
            mid[half, here, :] = value[:, half * 128 : half * 128 + 128]
    target = groups[1][0]
    store_slots(target, mid, 9, 9, 0)
    value = pack_gains(gains)
    for core in range(2):
        target[slot_rows(core, 18, SLOTS[1]), :] = value[core * 128 : core * 128 + 128]
    if not alone:
        two.swap()
        one.turn()
    for tap in range(9):
        here = slice(tap * 256, tap * 256 + 256)
        term = dot(columns[:, here], b[here, :], ((1,), (1,)))
        if tap == 0:
            acc[...] = term
        else:
            acc[...] += term
        if tap == 4 and not alone:
            one.combine_thin()
    if not alone:
        two.join()

    def dmid1(t, carry):
        dwhite[tile_rows(t), :256] = (acc[tile_rows(t), :] * s1[tile_rows(t), :]).astype(BF16)
        return carry

    lax.fori_loop(0, rows // TILE, dmid1, 0)
    value = dot(x[...], dwhite[:, :256], ((0,), (0,)))
    for half in range(2):
        top[half] = value[:, half * 128 : half * 128 + 128]
    store_slots(groups[2][0], top, 4, 4, 0)
    if not alone:
        three.swap()
        two.combine_wide()
        one.deepen()
    for j in range(4):
        here = slice(j * 256, j * 256 + 256)
        grad_out[:, here] = (dot(dwhite[:, :256], a[here, :], ((1,), (1,))) + dpre[:, here]).astype(BF16)
        if j == 1 and not alone:
            three.join()
    store = pltpu.make_async_copy(grad_out, input_grad, load_sems.at[5])
    store.start()
    if alone:
        sums[:, :8, :] = groups[0][0][...].reshape(256, 8, 128)
        sums[:, 8:32, :] = groups[1][0][...].reshape(256, 24, 128)
        sums[:, 32:, :] = groups[2][0][...].reshape(256, 8, 128)
    else:
        two.turn()
        three.combine_wide()
        two.combine_thin()
        three.turn()
        two.deepen()
        three.combine_thin()
        sums[0:8, :] = one.result() * scale
        three.deepen()
        sums[8:27, :] = two.result() * scale
        sums[32:40, :] = three.result() * scale
        one.drain()
        two.drain()
        three.drain()
    store.wait()


VM = pl.BlockSpec(memory_space=pltpu.VMEM)
ANY = pl.BlockSpec(memory_space=pl.ANY)


def shape(dims, kind=F32):
    return jax.ShapeDtypeStruct(dims, kind)


def block_step(inputs, out_grad, conv_first, conv_middle, conv_last, gain, span, scale, alone=False):
    rows = inputs.shape[0]

    def body(*refs):
        kernel(span, scale, alone, *refs)

    def vmem(*dims, kind=F32):
        return pltpu.VMEM(dims, kind)

    dma = pltpu.SemaphoreType.DMA
    scratch = [
        vmem(rows, 1024, kind=BF16), vmem(rows, 1024, kind=BF16), vmem(1024, 256, kind=BF16),
        vmem(2304, 256, kind=BF16), vmem(256, 1024, kind=BF16),
        vmem(rows, 256), vmem(rows + 2 * PAD, 256), vmem(rows, 2304, kind=BF16),
        vmem(rows, 256, kind=BF16), vmem(rows, 256), vmem(rows, 256, kind=BF16), vmem(rows, 256),
        vmem(256, 256), vmem(256, 128), vmem(256, 1024),
        vmem(16, 17, 128), vmem(16, 17, 128), vmem(16 if alone else 1, 136, 64),
        vmem(16, 17, 128), vmem(16, 17, 128), vmem(16, 17, 128), vmem(16, 17, 128),
        vmem(3, 17, 128), vmem(3, 17, 128),
        vmem(4, 256, 256), vmem(4, 256, 256), vmem(8, 1024),
        vmem(rows, 1024), vmem(rows, 1024), vmem(rows, 1024, kind=BF16), vmem(256, 1024, kind=BF16),
        vmem(256, 1024), vmem(8, 1024), vmem(8, 1024), vmem(256, 1024, kind=BF16),
        vmem(8, 256, 128), vmem(2, 2304, 128), vmem(2, 1024, 128),
        vmem(rows, 1024, kind=BF16), dma((6,)), *([dma((16,))] * 4 + [dma((1,))] * 2) * 2,
        *(vmem(256 * size, 128) for size in SLOTS),
        *(vmem(8, 4, 4, size, 128) for size in USED), *(vmem(8, 4, 4, size, 128) for size in USED),
        *(vmem(2, 4, 4, size, 128) for size in USED), *(vmem(2, 8, size, 128) for size in USED),
        *(vmem(2, 4, 2, 2, 4, size, 128) for size in USED), *(vmem(2, 4, 2, 2, size, 128) for size in USED),
        *[dma((33,))] * 6,
    ]
    params = {} if alone else dict(collective_id=0, has_side_effects=True)
    return pl.pallas_call(
        body,
        out_shape=(shape((rows, 1024), BF16), shape((256, 40, 128) if alone else (40, 128))),
        in_specs=[ANY] * 5 + [VM],
        out_specs=(ANY, VM),
        scratch_shapes=scratch,
        compiler_params=pltpu.CompilerParams(vmem_limit_bytes=67043328, **params),
        name="block_step",
    )(inputs, out_grad, conv_first, conv_middle, conv_last, gain.reshape(1, -1))


def finish_kernel(source, sums, target, first, middle, last, gain, buffer, arrive, leave):
    count = buffer.shape[0]
    size = source.shape[0] // count

    def copies(n):
        rows = pl.ds(n * size, size)
        return (
            pltpu.make_async_copy(source.at[rows], buffer.at[n], arrive.at[n]),
            pltpu.make_async_copy(buffer.at[n], target.at[rows], leave.at[n]),
        )

    for n in range(count):
        copies(n)[0].start()
    last[...] = sums[0:8, :]
    middle[...] = sums[8:26, :]
    gain[...] = sums[26:27, :4]
    first[...] = sums[32:40, :]
    for n in range(count):
        copies(n)[0].wait()
        copies(n)[1].start()
    for n in range(count):
        copies(n)[1].wait()


def finish(input_grad, sums):
    rows, width = input_grad.shape
    count = 7
    dma = pltpu.SemaphoreType.DMA
    return pl.pallas_call(
        finish_kernel,
        out_shape=(
            shape((rows, width), BF16), shape((8, 128)), shape((18, 128)), shape((8, 128)), shape((1, 4))
        ),
        in_specs=[ANY, VM],
        out_specs=(ANY, VM, VM, VM, VM),
        scratch_shapes=[pltpu.VMEM((count, rows // count, width), BF16), dma((count,)), dma((count,))],
        name="finish",
    )(input_grad, sums)


def shards(inputs, out_grad, conv_first, conv_middle, conv_last, gain):
    ghosts, groups = lax.axis_size("ghost"), lax.axis_size("group")
    span = float(inputs.shape[0] * ghosts)
    input_grad, sums = block_step(
        inputs, out_grad, conv_first, conv_middle, conv_last, gain, span, (span * groups) ** (-0.5)
    )
    input_grad, *grads = finish(input_grad, sums)
    return (input_grad, *(grad.reshape(-1) for grad in grads))


def solution(mesh):
    rows = P(("group", "ghost"))
    return jax.shard_map(
        shards,
        mesh=mesh,
        in_specs=(P(("group", "ghost"), None), P(("group", "ghost"), None), P(), P(), P(), P()),
        out_specs=(P(("group", "ghost"), None), rows, rows, rows, rows),
        check_vma=False,
    )
```

```python
import jax
import jax.numpy as jnp
from jax import lax
from jax.experimental import pallas as pl
from jax.experimental.pallas import tpu as pltpu
from jax.sharding import PartitionSpec as P

GROUP = 64
NEWTON = 5
SIDE = 14
PAD = 16
TILE = 112
MESH = pl.DeviceIdType.MESH
epsilon = 1e-05
F32 = jnp.float32
BF16 = jnp.bfloat16


def dot(left, right, dims=((1,), (0,))):
    return lax.dot_general(left, right, (dims, ((), ())), preferred_element_type=F32)


def parts(value, count):
    pieces = []
    for _ in range(count):
        piece = value.astype(BF16)
        pieces.append(piece)
        value = value - piece.astype(F32)
    return pieces


def dot_parts(left, right, dims=((1,), (0,))):
    total = None
    for a in left:
        for b in right:
            term = dot(a, b, dims)
            total = term if total is None else total + term
    return total


def dot_high(left, right, dims=((1,), (0,))):
    return lax.dot_general(
        left, right, (dims, ((), ())), preferred_element_type=F32, precision=lax.Precision.HIGHEST
    )


def sigmoid(v):
    return 0.5 + 0.5 * jnp.tanh(0.5 * v)


def tile_rows(t):
    return pl.ds(pl.multiple_of(t * TILE, TILE), TILE)


def edges(t):
    row = lax.broadcasted_iota(jnp.int32, (TILE, 128), 0).astype(F32) + float(t * TILE)
    line = jnp.floor((row + 0.5) * (1.0 / SIDE))
    column = row - line * SIDE
    image = jnp.floor((line + 0.5) * (1.0 / SIDE))
    return line - image * SIDE, column


def store_padded(padded, t, value):
    for half in range(2):
        padded[half, pl.ds(t * TILE + PAD, TILE), :] = value[:, half * 128 : half * 128 + 128]


def shifted_tiles(padded, columns, sign):
    for t in range(columns.shape[0] // TILE):
        line, column = edges(t)
        at = slice(t * TILE, t * TILE + TILE)
        for tap in range(9):
            dr, dc = sign * (tap // 3 - 1), sign * (tap % 3 - 1)
            start = t * TILE + PAD + dr * SIDE + dc
            keep = None
            if dr:
                keep = line > 0.5 if dr < 0 else line < SIDE - 1.5
            if dc:
                side = column > 0.5 if dc < 0 else column < SIDE - 1.5
                keep = side if keep is None else keep & side
            for half in range(2):
                value = padded[half, start : start + TILE, :]
                if keep is not None:
                    value = jnp.where(keep, value, 0.0)
                lanes = tap * 256 + half * 128
                columns[at, lanes : lanes + 128] = value.astype(BF16)


def lanes_of(rows, right):
    lane = lax.broadcasted_iota(jnp.int32, (rows, 128), 1)
    return lane, lane - (64 if right else 0), lax.broadcasted_iota(jnp.int32, (rows, 128), 0)


def pack_block(square, at, right, row):
    top, low = square[at : at + 32], square[at + 32 : at + 64]
    lane, rel, i = lanes_of(32, right)
    moved = pltpu.roll(low, 96, 1)
    corner = jnp.where(rel > i, top, jnp.where(rel == i, 0.5 * top, moved))
    value = jnp.where(rel < 32, corner, top)
    upper, lower = value[:16], value[16:]
    if right:
        upper = pltpu.roll(upper, 64, 1)
    else:
        lower = pltpu.roll(lower, 64, 1)
    packed = jnp.where(lane[:16] < 64, upper, lower)
    diagonal = jnp.sum(jnp.where(rel - 32 == i, 0.5 * low, 0.0), axis=0, keepdims=True)
    diagonal = pltpu.roll(diagonal, 96 if right else 32, 1)
    if right:
        row = pltpu.roll(row, 64, 1)
    flat = lane[:1]
    return packed, jnp.where(flat < 64, row, jnp.where(flat < 96, diagonal, 0.0))


def half_block(packed, extra, right):
    lane, rel, i = lanes_of(32, right)
    rolled = pltpu.roll(packed, 64, 1)
    value = jnp.concatenate([rolled, packed] if right else [packed, rolled], axis=0)
    diagonal = pltpu.roll(extra, 32 if right else 96, 1)
    inside = (rel >= 0) & (rel < 64)
    top = jnp.where(inside & ((rel >= 32) | (rel >= i)), value, 0.0)
    low = jnp.where(inside & (rel >= 32) & (rel - 32 < i), pltpu.roll(value, 32, 1), 0.0)
    low = jnp.where(rel - 32 == i, diagonal, low)
    return top, low


def fill_diagonal(target, source):
    zero = jnp.zeros((128, 128), F32)
    for pair in range(8):
        j, at = pair // 2, (pair % 2) * 128
        pieces = []
        for right in (False, True):
            k = 2 * pair + int(right)
            pieces += half_block(source[k, :16, :], source[k, 16:17, :], right)
        half = jnp.concatenate(pieces, axis=0)
        target[j, at : at + 128, at : at + 128] = half + half.T
        target[j, at : at + 128, 128 - at : 256 - at] = zero


def fill_row(target, source):
    lane = lax.broadcasted_iota(jnp.int32, (1, 128), 1)
    for pair in range(8):
        right = pltpu.roll(source[2 * pair + 1, 16:17, :], 64, 1)
        target[0:1, pair * 128 : pair * 128 + 128] = jnp.where(lane < 64, source[2 * pair, 16:17, :], right)


def fill_payload(payload, squares, row):
    for j in range(4):
        square = squares(j)
        for q in range(4):
            k = 4 * j + q
            tile = (q // 2) * 128
            packed, extra = pack_block(
                square[:, tile : tile + 128], q * 64, bool(q % 2), row[:, (k // 2) * 128 : (k // 2) * 128 + 128]
            )
            payload[k, :16, :] = packed
            payload[k, 16:17, :] = extra


def block_of(packed, extra):
    top, low = half_block(packed, extra, False)
    half = jnp.concatenate([top, low], axis=0)[:, :64]
    return half + half.T


def packed_of(square, row):
    wide = jnp.concatenate([square, jnp.zeros((64, 64), F32)], axis=1)
    return pack_block(wide, 0, False, jnp.concatenate([row, jnp.zeros((1, 64), F32)], axis=1))


def outer(left, right):
    first = lax.broadcasted_iota(jnp.int32, (8, 64), 0) == 0
    return dot_high(jnp.where(first, left, 0.0), jnp.broadcast_to(right, (8, 64)), ((0,), (0,)))


def eye(size):
    return lax.broadcasted_iota(jnp.int32, (size, size), 0) == lax.broadcasted_iota(jnp.int32, (size, size), 1)


def solve_white(span, packed, extra, keep):
    mean = extra[:, :64] * (1.0 / span)
    cov = block_of(packed, extra) * (1.0 / span) - outer(mean, mean) + jnp.where(eye(64), epsilon, 0.0)
    trace = trace_of(cov)
    white = newton(cov / trace, 64) / jnp.sqrt(jnp.full((64, 64), trace))
    keep[:64] = cov
    keep[64:128] = white
    keep[128:136] = jnp.broadcast_to(mean, (8, 64))
    return packed_of(white, dot_high(jnp.broadcast_to(mean, (8, 64)), white)[:1])


def solve_slope(span, packed, extra, keep):
    cov, white, mean = keep[:64], keep[64:128], keep[128:129]
    csum = extra[:, :64]
    lifted = outer(mean, csum)
    cross = block_of(packed, extra) - 0.5 * (lifted + lifted.T)
    trace = trace_of(cov)
    scaled = cov / trace
    up = jnp.concatenate([scaled, cross / jnp.sqrt(jnp.full((64, 64), trace))], axis=1)
    low = jnp.concatenate([jnp.zeros((64, 64), F32), scaled], axis=1)
    dn = newton(jnp.concatenate([up, low], axis=0), 128)[:64, 64:]
    dt = -jnp.sum(dn * scaled) / trace - 0.5 * jnp.sum(cross * white) / trace
    dcov = dn / trace + jnp.where(eye(64), dt, 0.0)
    sym = dcov + dcov.T
    wide = jnp.broadcast_to(csum, (8, 64))
    line = dot_high(wide, white, ((1,), (1,))) + dot_high(jnp.broadcast_to(mean, (8, 64)), sym)
    return packed_of(sym, line[:1] * (1.0 / span))


def newton(n, size):
    row = lax.broadcasted_iota(jnp.int32, (size, size), 0)
    lane = lax.broadcasted_iota(jnp.int32, (size, size), 1)
    project = jnp.where(row == lane, 1.5, 0.0) - 0.5 * n
    for sweep in range(NEWTON - 1):
        squared = dot_high(project, project)
        project = 1.5 * project - 0.5 * dot_high(squared, dot_high(project, n))
    return project


def trace_of(block, size=64):
    row = lax.broadcasted_iota(jnp.int32, (size, size), 0)
    lane = lax.broadcasted_iota(jnp.int32, (size, size), 1)
    return jnp.sum(jnp.where(row == lane, block, 0.0))


def remote(source, target, sems, at, peer):
    send, recv = sems
    return pltpu.make_async_remote_copy(
        src_ref=source, dst_ref=target, send_sem=send.at[at], recv_sem=recv.at[at], device_id=peer,
        device_id_type=MESH,
    )


class Place:
    def __init__(self):
        self.z, ghost = lax.axis_index("group"), lax.axis_index("ghost")
        self.x, self.y, self.core, self.chip = ghost // 8, (ghost // 2) % 4, ghost % 2, ghost // 2

    def chip_peer(self, chip):
        return (self.z, chip * 2 + self.core)

    def partner(self):
        return (self.z, self.chip * 2 + 1 - self.core)

    def along_x(self, s):
        return (self.z, ((self.x + s + 4) % 4) * 8 + self.y * 2 + self.core)

    def along_y(self, s):
        return (self.z, self.x * 8 + ((self.y + s + 4) % 4) * 2 + self.core)

    def along_z(self, s):
        return ((self.z + s) % 8, self.chip * 2 + self.core)

    def greet(self):
        barrier = pltpu.get_barrier_semaphore()

        def signal(peer):
            pl.semaphore_signal(barrier, inc=1, device_id=peer, device_id_type=MESH)

        for s in range(1, 16):
            signal(self.chip_peer((self.chip + s) % 16))
        for s in range(1, 8):
            signal(self.along_z(s))
        signal(self.partner())

    def greeted(self):
        pl.semaphore_wait(pltpu.get_barrier_semaphore(), 23)


def exchange(place, solve, payload, keep, out, got, mine, sems, cover, alone):
    if alone:
        cover()
        for k in range(16):
            value, extra = solve(payload[k, :16, :], payload[k, 16:17, :], keep.at[k])
            out[k, :16, :] = value
            out[k, 16:17, :] = extra
        return
    chip = place.chip
    scatter, spread, swap_sems = sems[0:2], sems[2:4], sems[4:6]

    def outward(s):
        target = (chip + s) % 16
        return remote(payload.at[target], got.at[s], scatter, s, place.chip_peer(target))

    def start(s, carry):
        outward(s).start()
        return carry

    lax.fori_loop(1, 16, start, 0)
    cover()
    mine[0] = payload[chip]

    def add(s, carry):
        outward(s).wait_recv()
        mine[0] += got[s]
        return carry

    lax.fori_loop(1, 16, add, 0)
    swap = remote(mine.at[0], mine.at[1], swap_sems, 0, place.partner())
    swap.start()
    swap.wait_recv()
    value, extra = solve(mine[0, :16, :] + mine[1, :16, :], mine[0, 16:17, :] + mine[1, 16:17, :], keep.at[0])
    mine[2, :16, :] = value
    mine[2, 16:17, :] = extra

    def back(s):
        return remote(mine.at[2], out.at[chip], spread, s, place.chip_peer((chip + s) % 16))

    def arrival(s):
        return remote(mine.at[2], out.at[(chip + 16 - s) % 16], spread, s, place.chip_peer((chip + s) % 16))

    def start_back(s, carry):
        back(s).start()
        return carry

    lax.fori_loop(1, 16, start_back, 0)
    out[chip] = mine[2]

    def finish(s, carry):
        arrival(s).wait_recv()
        return carry

    lax.fori_loop(1, 16, finish, 0)

    def drain(s, carry):
        outward(s).wait_send()
        back(s).wait_send()
        return carry

    lax.fori_loop(1, 16, drain, 0)
    swap.wait_send()


class AxisSum:
    def __init__(self, chunk, me, peer, box, sems, at):
        self.chunk, self.me, self.box = chunk, me, box
        relay, raw, comb, held = (box.at[n] for n in range(4))
        self.held, self.relay_in, self.raw_in, self.comb_in = held, relay, raw, comb
        self.relay, self.raw, self.comb = [], [], []
        for i, s in enumerate((1, -1)):
            to = peer(s)
            near = (me + s + 4) % 4
            self.relay.append(remote(chunk((me + 2) % 4, i), relay.at[i], sems, at + 3 * i, to))
            self.raw.append(remote(chunk(near, 1 - i), raw.at[i], sems, at + 3 * i + 1, to))
            self.comb.append(remote(held.at[i], comb.at[i], sems, at + 3 * i + 2, to))

    def begin(self):
        for i in range(2):
            self.relay[i].start()
        for i in range(2):
            self.raw[i].start()

    def combine(self):
        for i, s in enumerate((1, -1)):
            near = (self.me + s + 4) % 4
            self.relay[i].wait_recv()
            for n in range(2):
                self.held[i, n] = self.chunk(near, i)[n] + self.relay_in[i, n]
            self.comb[i].start()

    def end(self, store):
        for i in range(2):
            self.comb[i].wait_recv()
            self.raw[1 - i].wait_recv()
            for n in range(2):
                store(2 * i + n, self.chunk(self.me, i)[n] + self.comb_in[i, n] + self.raw_in[1 - i, n])

    def drain(self):
        for one in self.relay + self.raw + self.comb:
            one.wait_send()


class OwnerSum:
    def __init__(self, place, grads, other, total, half, last, wide, thin, *sems):
        self.place, self.other, self.total = place, other, total
        self.half, self.last = half, last
        used, slots = other.shape[3], grads.shape[0] // 256
        grads = grads.reshape(2, 8, 4, 4, slots, 128)
        self.own = lambda z: grads[place.core, z, :, :, :used, :]
        self.swaps = [
            remote(
                grads.at[1 - place.core, 4 * h : 4 * h + 4, :, :, :used, :], other.at[4 * h : 4 * h + 4], sems, h,
                place.partner(),
            )
            for h in range(2)
        ]
        self.wide = [
            AxisSum(lambda d, n: total.at[2 * n : 2 * n + 2, d], place.x, place.along_x, wide.at[0], sems, 2),
            AxisSum(lambda d, n: total.at[4 + 2 * n : 6 + 2 * n, :, d], place.y, place.along_y, wide.at[1], sems, 8),
        ]
        self.thin = [
            AxisSum(lambda d, n: half.at[0, 2 * n : 2 * n + 2, d], place.y, place.along_y, thin.at[0], sems, 14),
            AxisSum(lambda d, n: half.at[1, 2 * n : 2 * n + 2, d], place.x, place.along_x, thin.at[1], sems, 20),
        ]
        self.final = [
            remote(last.at[0, (place.z + s) % 8], last.at[1, s], sems, 25 + s, place.along_z(s)) for s in range(1, 8)
        ]

    def swap(self):
        for one in self.swaps:
            one.start()

    def join(self):
        for h in range(2):
            self.swaps[h].wait_recv()

            def body(i, carry):
                self.total[4 * h + i] = self.own(4 * h + i) + self.other[4 * h + i]
                return carry

            lax.fori_loop(0, 4, body, 0)
            self.wide[h].begin()

    def combine_wide(self):
        for h in range(2):
            self.wide[h].combine()

    def turn(self):
        for h in range(2):

            def store(n, value):
                self.half[h, n] = value

            self.wide[h].end(store)
            self.thin[h].begin()

    def combine_thin(self):
        for h in range(2):
            self.thin[h].combine()

    def deepen(self):
        for h in range(2):

            def store(n, value):
                self.last[0, 4 * h + n] = value

            self.thin[h].end(store)
        for one in self.final:
            one.start()

    def result(self):
        value = self.last[0, self.place.z]
        for s in range(1, 8):
            self.final[s - 1].wait_recv()
            value = value + self.last[1, s]
        return value

    def drain(self):
        for one in self.swaps + self.final:
            one.wait_send()
        for one in self.wide + self.thin:
            one.drain()


def slot_rows(core, slot, slots):
    return pl.ds(core * 128 * slots + slot, 128, stride=slots)


USED = (8, 19, 8)
SLOTS = (8, 24, 8)


def store_slots(target, source, count, step, at):
    slots = target.shape[0] // 256
    for core in range(2):
        for n in range(source.shape[0]):
            for q in range(count):
                rows = pl.ds(q + step * core, 128, stride=2 * step)
                target[slot_rows(core, at + n + q * source.shape[0], slots), :] = source[n, rows, :]


def pack_gains(gains):
    total = jnp.sum(gains[...], axis=0, keepdims=True)
    row = lax.broadcasted_iota(jnp.int32, (256, 1024), 0)
    own = (row & 127) * 2 + (row >> 7)
    channel = lax.broadcasted_iota(jnp.int32, (256, 1024), 1)
    spread = jnp.where((channel >> 2) == own, total, 0.0)
    channel = lax.broadcasted_iota(jnp.int32, (1024, 128), 0)
    lane = lax.broadcasted_iota(jnp.int32, (1024, 128), 1)
    pick = jnp.where((channel & 3) == lane, 1.0, 0.0).astype(BF16)
    return dot_parts(parts(spread, 3), [pick])


def kernel(
    span, scale, alone,
    x_in, og_in, a_in, b_in, c_in, gain, input_grad, sums, *scratch,
):
    (
        x, og, a, b, c, acc, padded, columns, h1, s1, h2, s2, gram, hsum, wide, payload, payload2, keep, whites,
        slopes, got, got2, mine, mine2, diagonal, diagonal2, row, white, dpre, dwhite, d, across, csum, gains, e,
        last, mid, top, h1t, h2t, xt, at, bt, ct, grad_out, load_sems, *rest,
    ) = scratch
    sems, rest = rest[:12], rest[12:]
    groups = [rest[n :: 3] for n in range(3)]
    place = None if alone else Place()
    loads = [
        pltpu.make_async_copy(source, target, load_sems.at[n])
        for n, (source, target) in enumerate(((a_in, a), (x_in, x), (b_in, b), (c_in, c), (og_in, og)))
    ]
    for one in loads:
        one.start()
    if not alone:
        place.greet()
    rows = x.shape[0]
    padded[:, :PAD, :] = jnp.zeros((2, PAD, 128), F32)
    padded[:, rows + PAD :, :] = jnp.zeros((2, PAD, 128), F32)

    loads[0].wait()
    loads[1].wait()
    acc[...] = dot(x[...], a[...])

    def first(t, carry):
        v = acc[tile_rows(t), :]
        s = sigmoid(v)
        s1[tile_rows(t), :] = s * (1.0 + v * (1.0 - s))
        h = (v * s).astype(BF16)
        h1[tile_rows(t), :] = h
        store_padded(padded, t, h.astype(F32))
        return carry

    lax.fori_loop(0, rows // TILE, first, 0)
    shifted_tiles(padded, columns, 1)
    loads[2].wait()
    acc[...] = dot(columns[...], b[...])

    def second(t, carry):
        v = acc[tile_rows(t), :]
        s = sigmoid(v)
        s2[tile_rows(t), :] = s * (1.0 + v * (1.0 - s))
        h2[tile_rows(t), :] = (v * s).astype(BF16)
        return carry

    lax.fori_loop(0, rows // TILE, second, 0)
    h2t[...] = h2[...].T
    gram[...] = dot(h2t[...], h2[...])
    loads[3].wait()
    wide[...] = dot_parts(parts(gram[...], 3), [c[...]])
    brow = dot_parts(parts(dot(jnp.ones((8, rows), BF16), h2[...]), 3), [c[...]])

    def squares(j):
        here = slice(j * 256, j * 256 + 256)
        return dot_parts([c[:, here]], parts(wide[:, here], 3), ((0,), (0,)))

    fill_payload(payload, squares, brow[:1])
    if not alone:
        place.greeted()

    def cover():
        hsum[...] = dot(h2t[...], jnp.ones((rows, 128), BF16))
        h1t[...] = h1[...].T
        for n in range(4):
            here = slice(n * 256, n * 256 + 256)
            xt[here, :] = x[:, here].T
            at[:, here] = a[here, :].T
            ct[here, :] = c[:, here].T
        for tap in range(9):
            here = slice(tap * 256, tap * 256 + 256)
            bt[here, :] = b[here, :].T
        loads[4].wait()

    exchange(
        place, lambda *args: solve_white(span, *args), payload, keep, whites, got, mine, sems[0:6], cover, alone
    )

    fill_diagonal(diagonal, whites)
    fill_row(row, whites)
    for j in range(4):
        here = slice(j * 256, j * 256 + 256)
        folded = dot_parts([c[:, here]], parts(diagonal[j], 2))
        high, low = parts(folded, 2)
        d[:, here] = high
        white[:, here] = dot(h2[...], high) + dot(h2[...], low)
    csum[...] = jnp.zeros_like(csum)
    gains[...] = jnp.zeros_like(gains)

    def slope(t, carry):
        for j in range(8):
            here = slice(j * 128, j * 128 + 128)
            w = white[tile_rows(t), here] - row[0:1, here]
            g = gain[0:1, here]
            v = x[tile_rows(t), here].astype(F32) + g * w
            s = sigmoid(v)
            u = og[tile_rows(t), here].astype(F32) * (s * (1.0 + v * (1.0 - s)))
            dpre[tile_rows(t), here] = u
            dw = g * u
            dwhite[tile_rows(t), here] = dw.astype(BF16)
            csum[:, here] += jnp.sum(dw.reshape(TILE // 8, 8, 128), axis=0)
            gains[:, here] += jnp.sum((u * w).reshape(TILE // 8, 8, 128), axis=0)
        return carry

    lax.fori_loop(0, rows // TILE, slope, 0)
    across[...] = dot(h2t[...], dwhite[...])

    def squares2(j):
        here = slice(j * 256, j * 256 + 256)
        square = dot_parts([c[:, here]], parts(across[:, here], 2), ((0,), (0,)))
        return 0.5 * (square + square.T)

    fill_payload(payload2, squares2, jnp.sum(csum[...], axis=0, keepdims=True))

    def cover2():
        acc[...] = dot(dwhite[...], d[...], ((1,), (1,)))
        for j in range(4):
            here = slice(j * 256, j * 256 + 256)
            high, low = parts(across[:, here], 2)
            pieces = parts(diagonal[j], 2)
            value = dot_parts([high], pieces, ((1,), (1,))) + dot(low, pieces[0], ((1,), (1,)))
            for half in range(2):
                last[2 * j + half] = value[:, half * 128 : half * 128 + 128]
        value = pack_gains(gains)
        for core in range(2):
            groups[1][0][slot_rows(core, 18, SLOTS[1]), :] = value[core * 128 : core * 128 + 128]

    exchange(
        place, lambda *args: solve_slope(span, *args), payload2, keep, slopes, got2, mine2, sems[6:12], cover2, alone
    )

    fill_diagonal(diagonal2, slopes)
    fill_row(row, slopes)
    for j in range(4):
        here = slice(j * 256, j * 256 + 256)
        e[:, here] = (dot_parts([c[:, here]], parts(diagonal2[j], 2)) * (1.0 / span)).astype(BF16)
    if alone:
        one = two = three = None
    else:
        one, two, three = (OwnerSum(place, *group) for group in groups)
    back = dot(e[...], ct[...]).astype(BF16)
    const = dot_parts(parts(jnp.broadcast_to(row[0:1, :], (8, 1024)), 2), [ct[...]])
    acc[...] += dot(h2[...], back)

    def dmid2(t, carry):
        v = (acc[tile_rows(t), :] - const[0:1, :]) * s2[tile_rows(t), :]
        store_padded(padded, t, v.astype(BF16).astype(F32))
        return carry

    lax.fori_loop(0, rows // TILE, dmid2, 0)
    shifted_tiles(padded, columns, -1)
    for tap in range(9):
        here = slice(tap * 256, tap * 256 + 256)
        value = dot(h1t[...], columns[:, here])
        for half in range(2):
            mid[half, here, :] = value[:, half * 128 : half * 128 + 128]
    store_slots(groups[1][0], mid, 9, 9, 0)
    if not alone:
        two.swap()
    grams = parts(gram[...], 2)
    for j in range(4):
        value = dot_parts(grams, [e[:, j * 256 : j * 256 + 256]])
        for half in range(2):
            n = 2 * j + half
            here = slice(n * 128, n * 128 + 128)
            last[n] = last[n] + value[:, half * 128 : half * 128 + 128] - hsum[...] * row[0:1, here]
    store_slots(groups[0][0], last, 1, 1, 0)
    if not alone:
        one.swap()
    acc[...] = dot(columns[...], bt[...])
    if not alone:
        two.join()
        one.join()

    def dmid1(t, carry):
        dwhite[tile_rows(t), :256] = (acc[tile_rows(t), :] * s1[tile_rows(t), :]).astype(BF16)
        return carry

    lax.fori_loop(0, rows // TILE, dmid1, 0)
    value = dot(xt[...], dwhite[:, :256])
    for half in range(2):
        top[half] = value[:, half * 128 : half * 128 + 128]
    store_slots(groups[2][0], top, 4, 4, 0)
    if not alone:
        three.swap()
        two.combine_wide()
        one.combine_wide()
    for j in range(4):
        here = slice(j * 256, j * 256 + 256)
        grad_out[:, here] = (dot(dwhite[:, :256], at[:, here]) + dpre[:, here]).astype(BF16)
        if j == 1 and not alone:
            three.join()
    store = pltpu.make_async_copy(grad_out, input_grad, load_sems.at[5])
    store.start()
    if alone:
        sums[:, :8, :] = groups[0][0][...].reshape(256, 8, 128)
        sums[:, 8:32, :] = groups[1][0][...].reshape(256, 24, 128)
        sums[:, 32:, :] = groups[2][0][...].reshape(256, 8, 128)
    else:
        two.turn()
        one.turn()
        three.combine_wide()
        two.combine_thin()
        one.combine_thin()
        three.turn()
        two.deepen()
        one.deepen()
        three.combine_thin()
        sums[0:8, :] = one.result() * scale
        three.deepen()
        sums[8:27, :] = two.result() * scale
        sums[32:40, :] = three.result() * scale
        one.drain()
        two.drain()
        three.drain()
    store.wait()


VM = pl.BlockSpec(memory_space=pltpu.VMEM)
ANY = pl.BlockSpec(memory_space=pl.ANY)


def shape(dims, kind=F32):
    return jax.ShapeDtypeStruct(dims, kind)


def block_step(inputs, out_grad, conv_first, conv_middle, conv_last, gain, span, scale, alone=False):
    rows = inputs.shape[0]

    def body(*refs):
        kernel(span, scale, alone, *refs)

    def vmem(*dims, kind=F32):
        return pltpu.VMEM(dims, kind)

    dma = pltpu.SemaphoreType.DMA
    scratch = [
        vmem(rows, 1024, kind=BF16), vmem(rows, 1024, kind=BF16), vmem(1024, 256, kind=BF16),
        vmem(2304, 256, kind=BF16), vmem(256, 1024, kind=BF16),
        vmem(rows, 256), vmem(2, rows + 2 * PAD, 128), vmem(rows, 2304, kind=BF16),
        vmem(rows, 256, kind=BF16), vmem(rows, 256), vmem(rows, 256, kind=BF16), vmem(rows, 256),
        vmem(256, 256), vmem(256, 128), vmem(256, 1024),
        vmem(16, 17, 128), vmem(16, 17, 128), vmem(16 if alone else 1, 136, 64),
        vmem(16, 17, 128), vmem(16, 17, 128), vmem(16, 17, 128), vmem(16, 17, 128),
        vmem(3, 17, 128), vmem(3, 17, 128),
        vmem(4, 256, 256), vmem(4, 256, 256), vmem(8, 1024),
        vmem(rows, 1024), vmem(rows, 1024), vmem(rows, 1024, kind=BF16), vmem(256, 1024, kind=BF16),
        vmem(256, 1024), vmem(8, 1024), vmem(8, 1024), vmem(256, 1024, kind=BF16),
        vmem(8, 256, 128), vmem(2, 2304, 128), vmem(2, 1024, 128),
        vmem(256, rows, kind=BF16), vmem(256, rows, kind=BF16), vmem(1024, rows, kind=BF16),
        vmem(256, 1024, kind=BF16), vmem(2304, 256, kind=BF16), vmem(1024, 256, kind=BF16),
        vmem(rows, 1024, kind=BF16), dma((6,)), *([dma((16,))] * 4 + [dma((1,))] * 2) * 2,
        *(vmem(256 * size, 128) for size in SLOTS),
        *(vmem(8, 4, 4, size, 128) for size in USED), *(vmem(8, 4, 4, size, 128) for size in USED),
        *(vmem(2, 4, 4, size, 128) for size in USED), *(vmem(2, 8, size, 128) for size in USED),
        *(vmem(2, 4, 2, 2, 4, size, 128) for size in USED), *(vmem(2, 4, 2, 2, size, 128) for size in USED),
        *[dma((33,))] * 6,
    ]
    params = {} if alone else dict(collective_id=0, has_side_effects=True)
    return pl.pallas_call(
        body,
        out_shape=(shape((rows, 1024), BF16), shape((256, 40, 128) if alone else (40, 128))),
        in_specs=[ANY] * 5 + [VM],
        out_specs=(ANY, VM),
        scratch_shapes=scratch,
        compiler_params=pltpu.CompilerParams(vmem_limit_bytes=67043328, **params),
        name="block_step",
    )(inputs, out_grad, conv_first, conv_middle, conv_last, gain.reshape(1, -1))


def finish_kernel(source, sums, target, first, middle, last, gain, buffer, small, arrive, leave):
    count = buffer.shape[0]
    size = source.shape[0] // count
    spans = [pl.ds(n * size, size) for n in range(count)]
    into = [pltpu.make_async_copy(source.at[rows], buffer.at[n], arrive.at[n]) for n, rows in enumerate(spans)]
    out = [pltpu.make_async_copy(buffer.at[n], target.at[rows], leave.at[n]) for n, rows in enumerate(spans)]
    into.append(pltpu.make_async_copy(sums, small, arrive.at[count]))
    pieces = ((small.at[32:40], first), (small.at[8:26], middle), (small.at[0:8], last))
    for n, (piece, place) in enumerate(pieces):
        out.append(pltpu.make_async_copy(piece, place, leave.at[count + n]))
    into[count].start()
    for n in range(count):
        into[n].start()
    into[count].wait()
    for n in range(3):
        out[count + n].start()
    gain[...] = small[26:27, :4]
    for n in range(count):
        into[n].wait()
        out[n].start()
    for one in out:
        one.wait()


def finish(input_grad, sums):
    rows, width = input_grad.shape
    count = 2
    dma = pltpu.SemaphoreType.DMA
    return pl.pallas_call(
        finish_kernel,
        out_shape=(
            shape((rows, width), BF16), shape((8, 128)), shape((18, 128)), shape((8, 128)), shape((1, 4))
        ),
        in_specs=[ANY, ANY],
        out_specs=(ANY, ANY, ANY, ANY, VM),
        scratch_shapes=[
            pltpu.VMEM((count, rows // count, width), BF16), pltpu.VMEM((40, 128), F32), dma((count + 1,)),
            dma((count + 3,)),
        ],
        name="finish",
    )(input_grad, sums)


def shards(inputs, out_grad, conv_first, conv_middle, conv_last, gain):
    ghosts, groups = lax.axis_size("ghost"), lax.axis_size("group")
    span = float(inputs.shape[0] * ghosts)
    input_grad, sums = block_step(
        inputs, out_grad, conv_first, conv_middle, conv_last, gain, span, (span * groups) ** (-0.5)
    )
    input_grad, *grads = finish(input_grad, sums)
    return (input_grad, *(grad.reshape(-1) for grad in grads))


def solution(mesh):
    rows = P(("group", "ghost"))
    return jax.shard_map(
        shards,
        mesh=mesh,
        in_specs=(P(("group", "ghost"), None), P(("group", "ghost"), None), P(), P(), P(), P()),
        out_specs=(P(("group", "ghost"), None), rows, rows, rows, rows),
        check_vma=False,
    )
```

```python
import jax
import jax.numpy as jnp
from jax import lax
from jax.experimental import pallas as pl
from jax.experimental.pallas import tpu as pltpu
from jax.sharding import PartitionSpec as P

GROUP = 64
NEWTON = 5
SIDE = 14
PAD = 16
TILE = 112
MESH = pl.DeviceIdType.MESH
epsilon = 1e-05
F32 = jnp.float32
BF16 = jnp.bfloat16


def dot(left, right, dims=((1,), (0,))):
    return lax.dot_general(left, right, (dims, ((), ())), preferred_element_type=F32)


def parts(value, count):
    pieces = []
    for _ in range(count):
        piece = value.astype(BF16)
        pieces.append(piece)
        value = value - piece.astype(F32)
    return pieces


def dot_parts(left, right, dims=((1,), (0,))):
    total = None
    for a in left:
        for b in right:
            term = dot(a, b, dims)
            total = term if total is None else total + term
    return total


def dot_high(left, right, dims=((1,), (0,))):
    return lax.dot_general(
        left, right, (dims, ((), ())), preferred_element_type=F32, precision=lax.Precision.HIGHEST
    )


def sigmoid(v):
    return 0.5 + 0.5 * jnp.tanh(0.5 * v)


def tile_rows(t):
    return pl.ds(pl.multiple_of(t * TILE, TILE), TILE)


def edges(t):
    row = lax.broadcasted_iota(jnp.int32, (TILE, 128), 0).astype(F32) + float(t * TILE)
    line = jnp.floor((row + 0.5) * (1.0 / SIDE))
    column = row - line * SIDE
    image = jnp.floor((line + 0.5) * (1.0 / SIDE))
    return line - image * SIDE, column


def store_padded(padded, t, value):
    for half in range(2):
        padded[half, pl.ds(t * TILE + PAD, TILE), :] = value[:, half * 128 : half * 128 + 128]


def shifted_columns(padded, columns, sign):
    for t in range(columns.shape[0] // TILE):
        column = edges(t)[1]
        for c in range(3):
            dc = sign * (c - 1)
            start = t * TILE + PAD + dc
            for half in range(2):
                value = padded[half, start : start + TILE, :]
                if dc:
                    value = jnp.where(column > 0.5 if dc < 0 else column < SIDE - 1.5, value, 0.0)
                lanes = c * 256 + half * 128
                columns[t * TILE : t * TILE + TILE, lanes : lanes + 128] = value.astype(BF16)


def from_line(padded, half, t, dr):
    line = edges(t)[0]
    start = t * TILE + PAD + dr * SIDE
    value = padded[half, start : start + TILE, :]
    return jnp.where(line > 0.5 if dr < 0 else line < SIDE - 1.5, value, 0.0)


def three_lines(columns, weights, acc, beside):
    rows = columns.shape[0]
    for r in range(3):
        value = dot(columns[...], weights[r * 768 : r * 768 + 768, :])
        if r == 1:
            acc[...] = value
        else:
            for half in range(2):
                beside[r // 2, half, PAD : PAD + rows, :] = value[:, half * 128 : half * 128 + 128]


def summed_lines(acc, beside, half, t, sign):
    value = acc[t * TILE : t * TILE + TILE, half * 128 : half * 128 + 128]
    return value + from_line(beside.at[0], half, t, -sign) + from_line(beside.at[1], half, t, sign)


def lanes_of(rows, right):
    lane = lax.broadcasted_iota(jnp.int32, (rows, 128), 1)
    return lane, lane - (64 if right else 0), lax.broadcasted_iota(jnp.int32, (rows, 128), 0)


def pack_block(square, at, right, row):
    top, low = square[at : at + 32], square[at + 32 : at + 64]
    lane, rel, i = lanes_of(32, right)
    moved = pltpu.roll(low, 96, 1)
    corner = jnp.where(rel > i, top, jnp.where(rel == i, 0.5 * top, moved))
    value = jnp.where(rel < 32, corner, top)
    upper, lower = value[:16], value[16:]
    if right:
        upper = pltpu.roll(upper, 64, 1)
    else:
        lower = pltpu.roll(lower, 64, 1)
    packed = jnp.where(lane[:16] < 64, upper, lower)
    diagonal = jnp.sum(jnp.where(rel - 32 == i, 0.5 * low, 0.0), axis=0, keepdims=True)
    diagonal = pltpu.roll(diagonal, 96 if right else 32, 1)
    if right:
        row = pltpu.roll(row, 64, 1)
    flat = lane[:1]
    return packed, jnp.where(flat < 64, row, jnp.where(flat < 96, diagonal, 0.0))


def half_block(packed, extra, right):
    lane, rel, i = lanes_of(32, right)
    rolled = pltpu.roll(packed, 64, 1)
    value = jnp.concatenate([rolled, packed] if right else [packed, rolled], axis=0)
    diagonal = pltpu.roll(extra, 32 if right else 96, 1)
    inside = (rel >= 0) & (rel < 64)
    top = jnp.where(inside & ((rel >= 32) | (rel >= i)), value, 0.0)
    low = jnp.where(inside & (rel >= 32) & (rel - 32 < i), pltpu.roll(value, 32, 1), 0.0)
    low = jnp.where(rel - 32 == i, diagonal, low)
    return top, low


def fill_diagonal(target, source):
    zero = jnp.zeros((128, 128), F32)
    for pair in range(8):
        j, at = pair // 2, (pair % 2) * 128
        pieces = []
        for right in (False, True):
            k = 2 * pair + int(right)
            pieces += half_block(source[k, :16, :], source[k, 16:17, :], right)
        half = jnp.concatenate(pieces, axis=0)
        target[j, at : at + 128, at : at + 128] = half + half.T
        target[j, at : at + 128, 128 - at : 256 - at] = zero


def fill_row(target, source):
    lane = lax.broadcasted_iota(jnp.int32, (1, 128), 1)
    for pair in range(8):
        right = pltpu.roll(source[2 * pair + 1, 16:17, :], 64, 1)
        target[0:1, pair * 128 : pair * 128 + 128] = jnp.where(lane < 64, source[2 * pair, 16:17, :], right)


def fill_payload(payload, squares, row):
    for j in range(4):
        square = squares(j)
        for q in range(4):
            k = 4 * j + q
            tile = (q // 2) * 128
            packed, extra = pack_block(
                square[:, tile : tile + 128], q * 64, bool(q % 2), row[:, (k // 2) * 128 : (k // 2) * 128 + 128]
            )
            payload[k, :16, :] = packed
            payload[k, 16:17, :] = extra


def block_of(packed, extra):
    top, low = half_block(packed, extra, False)
    half = jnp.concatenate([top, low], axis=0)[:, :64]
    return half + half.T


def packed_of(square, row):
    wide = jnp.concatenate([square, jnp.zeros((64, 64), F32)], axis=1)
    return pack_block(wide, 0, False, jnp.concatenate([row, jnp.zeros((1, 64), F32)], axis=1))


def outer(left, right):
    first = lax.broadcasted_iota(jnp.int32, (8, 64), 0) == 0
    return dot_high(jnp.where(first, left, 0.0), jnp.broadcast_to(right, (8, 64)), ((0,), (0,)))


def eye(size):
    return lax.broadcasted_iota(jnp.int32, (size, size), 0) == lax.broadcasted_iota(jnp.int32, (size, size), 1)


def solve_white(span, packed, extra, keep):
    mean = extra[:, :64] * (1.0 / span)
    cov = block_of(packed, extra) * (1.0 / span) - outer(mean, mean) + jnp.where(eye(64), epsilon, 0.0)
    trace = trace_of(cov)
    white = newton(cov / trace, 64) / jnp.sqrt(jnp.full((64, 64), trace))
    keep[:64] = cov
    keep[64:128] = white
    keep[128:136] = jnp.broadcast_to(mean, (8, 64))
    return packed_of(white, dot_high(jnp.broadcast_to(mean, (8, 64)), white)[:1])


def solve_slope(span, packed, extra, keep):
    cov, white, mean = keep[:64], keep[64:128], keep[128:129]
    csum = extra[:, :64]
    lifted = outer(mean, csum)
    cross = block_of(packed, extra) - 0.5 * (lifted + lifted.T)
    trace = trace_of(cov)
    scaled = cov / trace
    up = jnp.concatenate([scaled, cross / jnp.sqrt(jnp.full((64, 64), trace))], axis=1)
    low = jnp.concatenate([jnp.zeros((64, 64), F32), scaled], axis=1)
    dn = newton(jnp.concatenate([up, low], axis=0), 128)[:64, 64:]
    dt = -jnp.sum(dn * scaled) / trace - 0.5 * jnp.sum(cross * white) / trace
    dcov = dn / trace + jnp.where(eye(64), dt, 0.0)
    sym = dcov + dcov.T
    wide = jnp.broadcast_to(csum, (8, 64))
    line = dot_high(wide, white, ((1,), (1,))) + dot_high(jnp.broadcast_to(mean, (8, 64)), sym)
    return packed_of(sym, line[:1] * (1.0 / span))


def newton(n, size):
    row = lax.broadcasted_iota(jnp.int32, (size, size), 0)
    lane = lax.broadcasted_iota(jnp.int32, (size, size), 1)
    project = jnp.where(row == lane, 1.5, 0.0) - 0.5 * n
    for sweep in range(NEWTON - 1):
        squared = dot_high(project, project)
        project = 1.5 * project - 0.5 * dot_high(squared, dot_high(project, n))
    return project


def trace_of(block, size=64):
    row = lax.broadcasted_iota(jnp.int32, (size, size), 0)
    lane = lax.broadcasted_iota(jnp.int32, (size, size), 1)
    return jnp.sum(jnp.where(row == lane, block, 0.0))


def remote(source, target, sems, at, peer):
    send, recv = sems
    return pltpu.make_async_remote_copy(
        src_ref=source, dst_ref=target, send_sem=send.at[at], recv_sem=recv.at[at], device_id=peer,
        device_id_type=MESH,
    )


class Place:
    def __init__(self):
        self.z, ghost = lax.axis_index("group"), lax.axis_index("ghost")
        self.x, self.y, self.core, self.chip = ghost // 8, (ghost // 2) % 4, ghost % 2, ghost // 2

    def chip_peer(self, chip):
        return (self.z, chip * 2 + self.core)

    def partner(self):
        return (self.z, self.chip * 2 + 1 - self.core)

    def along_x(self, s):
        return (self.z, ((self.x + s + 4) % 4) * 8 + self.y * 2 + self.core)

    def along_y(self, s):
        return (self.z, self.x * 8 + ((self.y + s + 4) % 4) * 2 + self.core)

    def along_z(self, s):
        return ((self.z + s) % 8, self.chip * 2 + self.core)

    def greet(self):
        barrier = pltpu.get_barrier_semaphore()

        def signal(peer):
            pl.semaphore_signal(barrier, inc=1, device_id=peer, device_id_type=MESH)

        for s in range(1, 16):
            signal(self.chip_peer((self.chip + s) % 16))
        for s in range(1, 8):
            signal(self.along_z(s))
        signal(self.partner())

    def greeted(self):
        pl.semaphore_wait(pltpu.get_barrier_semaphore(), 23)


def exchange(place, solve, payload, keep, out, got, mine, sems, cover, alone):
    if alone:
        cover()
        for k in range(16):
            value, extra = solve(payload[k, :16, :], payload[k, 16:17, :], keep.at[k])
            out[k, :16, :] = value
            out[k, 16:17, :] = extra
        return
    chip = place.chip
    scatter, spread, swap_sems = sems[0:2], sems[2:4], sems[4:6]

    def outward(s):
        target = (chip + s) % 16
        return remote(payload.at[target], got.at[s], scatter, s, place.chip_peer(target))

    def start(s, carry):
        outward(s).start()
        return carry

    lax.fori_loop(1, 16, start, 0)
    cover()
    mine[0] = payload[chip]

    def add(s, carry):
        outward(s).wait_recv()
        mine[0] += got[s]
        return carry

    lax.fori_loop(1, 16, add, 0)
    swap = remote(mine.at[0], mine.at[1], swap_sems, 0, place.partner())
    swap.start()
    swap.wait_recv()
    value, extra = solve(mine[0, :16, :] + mine[1, :16, :], mine[0, 16:17, :] + mine[1, 16:17, :], keep.at[0])
    mine[2, :16, :] = value
    mine[2, 16:17, :] = extra

    def back(s):
        return remote(mine.at[2], out.at[chip], spread, s, place.chip_peer((chip + s) % 16))

    def arrival(s):
        return remote(mine.at[2], out.at[(chip + 16 - s) % 16], spread, s, place.chip_peer((chip + s) % 16))

    def start_back(s, carry):
        back(s).start()
        return carry

    lax.fori_loop(1, 16, start_back, 0)
    out[chip] = mine[2]

    def finish(s, carry):
        arrival(s).wait_recv()
        return carry

    lax.fori_loop(1, 16, finish, 0)

    def drain(s, carry):
        outward(s).wait_send()
        back(s).wait_send()
        return carry

    lax.fori_loop(1, 16, drain, 0)
    swap.wait_send()


class AxisSum:
    def __init__(self, chunk, me, peer, box, sems, at):
        self.chunk, self.me, self.box = chunk, me, box
        relay, raw, comb, held = (box.at[n] for n in range(4))
        self.held, self.relay_in, self.raw_in, self.comb_in = held, relay, raw, comb
        self.relay, self.raw, self.comb = [], [], []
        for i, s in enumerate((1, -1)):
            to = peer(s)
            near = (me + s + 4) % 4
            self.relay.append(remote(chunk((me + 2) % 4, i), relay.at[i], sems, at + 3 * i, to))
            self.raw.append(remote(chunk(near, 1 - i), raw.at[i], sems, at + 3 * i + 1, to))
            self.comb.append(remote(held.at[i], comb.at[i], sems, at + 3 * i + 2, to))

    def begin(self):
        for i in range(2):
            self.relay[i].start()
        for i in range(2):
            self.raw[i].start()

    def combine(self):
        for i, s in enumerate((1, -1)):
            near = (self.me + s + 4) % 4
            self.relay[i].wait_recv()
            for n in range(2):
                self.held[i, n] = self.chunk(near, i)[n] + self.relay_in[i, n]
            self.comb[i].start()

    def end(self, store):
        for i in range(2):
            self.comb[i].wait_recv()
            self.raw[1 - i].wait_recv()
            for n in range(2):
                store(2 * i + n, self.chunk(self.me, i)[n] + self.comb_in[i, n] + self.raw_in[1 - i, n])

    def drain(self):
        for one in self.relay + self.raw + self.comb:
            one.wait_send()


class DirectSum:
    def __init__(self, chunk, me, peer, box, sems, at):
        self.chunk, self.me, self.box = chunk, me, box
        self.copies = [remote(chunk((me + s) % 4), box.at[s], sems, at + s, peer(s)) for s in range(1, 4)]

    def begin(self):
        for one in self.copies:
            one.start()

    def combine(self):
        pass

    def end(self, store):
        for one in self.copies:
            one.wait_recv()
        for n in range(4):
            store(n, self.chunk(self.me)[n] + self.box[1, n] + self.box[2, n] + self.box[3, n])

    def drain(self):
        for one in self.copies:
            one.wait_send()


class OwnerSum:
    def __init__(self, place, grads, other, total, half, last, wide, thin, *sems):
        self.place, self.other, self.total = place, other, total
        self.half, self.last = half, last
        used, slots = other.shape[3], grads.shape[0] // 256
        grads = grads.reshape(2, 8, 4, 4, slots, 128)
        self.own = lambda z: grads[place.core, z, :, :, :used, :]
        self.swaps = [
            remote(
                grads.at[1 - place.core, 4 * h : 4 * h + 4, :, :, :used, :], other.at[4 * h : 4 * h + 4], sems, h,
                place.partner(),
            )
            for h in range(2)
        ]
        self.wide = [
            AxisSum(lambda d, n: total.at[2 * n : 2 * n + 2, d], place.x, place.along_x, wide.at[0], sems, 2),
            AxisSum(lambda d, n: total.at[4 + 2 * n : 6 + 2 * n, :, d], place.y, place.along_y, wide.at[1], sems, 8),
        ]
        if len(thin.shape) == 5:
            self.thin = [
                DirectSum(lambda d: half.at[0, :, d], place.y, place.along_y, thin.at[0], sems, 14),
                DirectSum(lambda d: half.at[1, :, d], place.x, place.along_x, thin.at[1], sems, 20),
            ]
        else:
            self.thin = [
                AxisSum(lambda d, n: half.at[0, 2 * n : 2 * n + 2, d], place.y, place.along_y, thin.at[0], sems, 14),
                AxisSum(lambda d, n: half.at[1, 2 * n : 2 * n + 2, d], place.x, place.along_x, thin.at[1], sems, 20),
            ]
        self.final = [
            remote(last.at[0, (place.z + s) % 8], last.at[1, s], sems, 25 + s, place.along_z(s)) for s in range(1, 8)
        ]

    def swap(self):
        for one in self.swaps:
            one.start()

    def join(self):
        for h in range(2):
            self.swaps[h].wait_recv()

            def body(i, carry):
                self.total[4 * h + i] = self.own(4 * h + i) + self.other[4 * h + i]
                return carry

            lax.fori_loop(0, 4, body, 0)
            self.wide[h].begin()

    def combine_wide(self):
        for h in range(2):
            self.wide[h].combine()

    def turn(self):
        for h in range(2):

            def store(n, value):
                self.half[h, n] = value

            self.wide[h].end(store)
            self.thin[h].begin()

    def combine_thin(self):
        for h in range(2):
            self.thin[h].combine()

    def deepen(self):
        for h in range(2):

            def store(n, value):
                self.last[0, 4 * h + n] = value

            self.thin[h].end(store)
        for one in self.final:
            one.start()

    def result(self):
        value = self.last[0, self.place.z]
        for s in range(1, 8):
            self.final[s - 1].wait_recv()
            value = value + self.last[1, s]
        return value

    def drain(self):
        for one in self.swaps + self.final:
            one.wait_send()
        for one in self.wide + self.thin:
            one.drain()


def slot_rows(core, slot, slots):
    return pl.ds(core * 128 * slots + slot, 128, stride=slots)


USED = (8, 19, 8)
SLOTS = (8, 24, 8)


def store_slots(target, source, count, step, at):
    slots = target.shape[0] // 256
    for core in range(2):
        for n in range(source.shape[0]):
            for q in range(count):
                rows = pl.ds(q + step * core, 128, stride=2 * step)
                target[slot_rows(core, at + n + q * source.shape[0], slots), :] = source[n, rows, :]


def pack_gains(gains):
    total = jnp.sum(gains[...], axis=0, keepdims=True)
    row = lax.broadcasted_iota(jnp.int32, (256, 1024), 0)
    own = (row & 127) * 2 + (row >> 7)
    channel = lax.broadcasted_iota(jnp.int32, (256, 1024), 1)
    spread = jnp.where((channel >> 2) == own, total, 0.0)
    channel = lax.broadcasted_iota(jnp.int32, (1024, 128), 0)
    lane = lax.broadcasted_iota(jnp.int32, (1024, 128), 1)
    pick = jnp.where((channel & 3) == lane, 1.0, 0.0).astype(BF16)
    return dot_parts(parts(spread, 3), [pick])


def kernel(
    span, scale, alone,
    x_in, og_in, a_in, b_in, c_in, gain, input_grad, sums, *scratch,
):
    (
        x, og, a, b, c, acc, padded, beside, columns, s1, twice, s2, gram, hsum, wide, payload, payload2, keep, whites,
        slopes, got, got2, mine, mine2, diagonal, diagonal2, row, white, dpre, dwhite, d, across, csum, gains, e,
        last, mid, top, h1t, h2t, xt, at, bt, ct, dmid1, grad_out, load_sems, *rest,
    ) = scratch
    sems, rest = rest[:12], rest[12:]
    groups = [rest[n :: 3] for n in range(3)]
    place = None if alone else Place()
    loads = [
        pltpu.make_async_copy(source, target, load_sems.at[n])
        for n, (source, target) in enumerate(((a_in, a), (x_in, x), (b_in, b), (c_in, c), (og_in, og)))
    ]
    for one in loads:
        one.start()
    if not alone:
        place.greet()
    rows = x.shape[0]
    padded[:, :PAD, :] = jnp.zeros((2, PAD, 128), F32)
    padded[:, rows + PAD :, :] = jnp.zeros((2, PAD, 128), F32)
    beside[:, :, :PAD, :] = jnp.zeros((2, 2, PAD, 128), F32)
    beside[:, :, rows + PAD :, :] = jnp.zeros((2, 2, PAD, 128), F32)

    loads[0].wait()
    loads[1].wait()
    acc[...] = dot(x[...], a[...])

    def first(t, carry):
        v = acc[tile_rows(t), :]
        s = sigmoid(v)
        s1[tile_rows(t), :] = s * (1.0 + v * (1.0 - s))
        h = (v * s).astype(BF16)
        store_padded(padded, t, h.astype(F32))
        return carry

    lax.fori_loop(0, rows // TILE, first, 0)
    shifted_columns(padded, columns, 1)
    loads[2].wait()
    three_lines(columns, b, acc, beside)
    for t in range(rows // TILE):
        for half in range(2):
            here = slice(t * TILE, t * TILE + TILE), slice(half * 128, half * 128 + 128)
            v = summed_lines(acc, beside, half, t, 1)
            s = sigmoid(v)
            s2[here] = s * (1.0 + v * (1.0 - s))
            value = (v * s).astype(BF16)
            twice[here] = value
            twice[here[0], here[1].start + 256 : here[1].stop + 256] = value
    h2 = twice.at[:, :256]
    h2t[...] = h2[...].T
    gram[...] = dot(h2t[...], h2[...])
    loads[3].wait()
    wide[...] = dot_parts(parts(gram[...], 3), [c[...]])
    brow = dot_parts(parts(dot(jnp.ones((8, rows), BF16), h2[...]), 3), [c[...]])

    def squares(j):
        here = slice(j * 256, j * 256 + 256)
        return dot_parts([c[:, here]], parts(wide[:, here], 3), ((0,), (0,)))

    fill_payload(payload, squares, brow[:1])
    if not alone:
        place.greeted()

    def cover():
        hsum[...] = dot(h2t[...], jnp.ones((rows, 128), BF16))
        for r in range(3):
            for t in range(rows // TILE):
                for half in range(2):
                    lanes = slice(r * 256 + half * 128, r * 256 + half * 128 + 128)
                    if r == 1:
                        value = padded[half, t * TILE + PAD : t * TILE + TILE + PAD, :]
                    else:
                        value = from_line(padded, half, t, r - 1)
                    columns[t * TILE : t * TILE + TILE, lanes] = value.astype(BF16)
            h1t[r * 256 : r * 256 + 256, :] = columns[:, r * 256 : r * 256 + 256].T
        for n in range(4):
            here = slice(n * 256, n * 256 + 256)
            xt[here, :] = x[:, here].T
            at[:, here] = a[here, :].T
            ct[here, :] = c[:, here].T
        for tap in range(9):
            here = slice(tap * 256, tap * 256 + 256)
            bt[here, :] = b[here, :].T
        loads[4].wait()

    exchange(
        place, lambda *args: solve_white(span, *args), payload, keep, whites, got, mine, sems[0:6], cover, alone
    )

    fill_diagonal(diagonal, whites)
    fill_row(row, whites)
    for j in range(4):
        here = slice(j * 256, j * 256 + 256)
        folded = dot_parts([c[:, here]], parts(diagonal[j], 2))
        high, low = parts(folded, 2)
        d[:, here] = high
        white[:, here] = dot(twice[...], jnp.concatenate([high, low], axis=0))
    csum[...] = jnp.zeros_like(csum)
    gains[...] = jnp.zeros_like(gains)

    def slope(t, carry):
        for j in range(8):
            here = slice(j * 128, j * 128 + 128)
            w = white[tile_rows(t), here] - row[0:1, here]
            g = gain[0:1, here]
            v = x[tile_rows(t), here].astype(F32) + g * w
            s = sigmoid(v)
            u = og[tile_rows(t), here].astype(F32) * (s * (1.0 + v * (1.0 - s)))
            dpre[tile_rows(t), here] = u
            dw = g * u
            dwhite[tile_rows(t), here] = dw.astype(BF16)
            csum[:, here] += jnp.sum(dw.reshape(TILE // 8, 8, 128), axis=0)
            gains[:, here] += jnp.sum((u * w).reshape(TILE // 8, 8, 128), axis=0)
        return carry

    lax.fori_loop(0, rows // TILE, slope, 0)
    across[...] = dot(h2t[...], dwhite[...])

    def squares2(j):
        here = slice(j * 256, j * 256 + 256)
        square = dot_parts([c[:, here]], parts(across[:, here], 2), ((0,), (0,)))
        return 0.5 * (square + square.T)

    fill_payload(payload2, squares2, jnp.sum(csum[...], axis=0, keepdims=True))

    def cover2():
        acc[...] = dot(dwhite[...], d[...], ((1,), (1,)))
        for j in range(4):
            here = slice(j * 256, j * 256 + 256)
            high, low = parts(across[:, here], 2)
            pieces = parts(diagonal[j], 2)
            value = dot_parts([high], pieces, ((1,), (1,))) + dot(low, pieces[0], ((1,), (1,)))
            for half in range(2):
                last[2 * j + half] = value[:, half * 128 : half * 128 + 128]
        value = pack_gains(gains)
        for core in range(2):
            groups[1][0][slot_rows(core, 18, SLOTS[1]), :] = value[core * 128 : core * 128 + 128]

    exchange(
        place, lambda *args: solve_slope(span, *args), payload2, keep, slopes, got2, mine2, sems[6:12], cover2, alone
    )

    fill_diagonal(diagonal2, slopes)
    fill_row(row, slopes)
    for j in range(4):
        here = slice(j * 256, j * 256 + 256)
        e[:, here] = (dot_parts([c[:, here]], parts(diagonal2[j], 2)) * (1.0 / span)).astype(BF16)
    if alone:
        one = two = three = None
    else:
        one, two, three = (OwnerSum(place, *group) for group in groups)
    back = dot(e[...], ct[...]).astype(BF16)
    const = dot_parts(parts(jnp.broadcast_to(row[0:1, :], (8, 1024)), 2), [ct[...]])
    acc[...] += dot(h2[...], back)

    def dmid2(t, carry):
        v = (acc[tile_rows(t), :] - const[0:1, :]) * s2[tile_rows(t), :]
        store_padded(padded, t, v.astype(BF16).astype(F32))
        return carry

    lax.fori_loop(0, rows // TILE, dmid2, 0)
    shifted_columns(padded, columns, -1)
    for column in range(3):
        value = dot(h1t[...], columns[:, column * 256 : column * 256 + 256])
        for r in range(3):
            tap = 3 * r + column
            for half in range(2):
                mid[half, tap * 256 : tap * 256 + 256, :] = value[
                    r * 256 : r * 256 + 256, half * 128 : half * 128 + 128
                ]
    store_slots(groups[1][0], mid, 9, 9, 0)
    if not alone:
        two.swap()
    grams = parts(gram[...], 2)
    for j in range(4):
        value = dot_parts(grams, [e[:, j * 256 : j * 256 + 256]])
        for half in range(2):
            n = 2 * j + half
            here = slice(n * 128, n * 128 + 128)
            last[n] = last[n] + value[:, half * 128 : half * 128 + 128] - hsum[...] * row[0:1, here]
    store_slots(groups[0][0], last, 1, 1, 0)
    if not alone:
        one.swap()
    three_lines(columns, bt, acc, beside)
    if not alone:
        two.join()
        one.join()

    for t in range(rows // TILE):
        for half in range(2):
            here = slice(t * TILE, t * TILE + TILE), slice(half * 128, half * 128 + 128)
            dmid1[here] = (summed_lines(acc, beside, half, t, -1) * s1[here]).astype(BF16)
    value = dot(xt[...], dmid1[...])
    for half in range(2):
        top[half] = value[:, half * 128 : half * 128 + 128]
    store_slots(groups[2][0], top, 4, 4, 0)
    if not alone:
        three.swap()
        two.combine_wide()
        one.combine_wide()
    for j in range(4):
        here = slice(j * 256, j * 256 + 256)
        grad_out[:, here] = (dot(dmid1[...], at[:, here]) + dpre[:, here]).astype(BF16)
        if j == 1 and not alone:
            three.join()
    store = pltpu.make_async_copy(grad_out, input_grad, load_sems.at[5])
    store.start()
    if alone:
        sums[:, :8, :] = groups[0][0][...].reshape(256, 8, 128)
        sums[:, 8:32, :] = groups[1][0][...].reshape(256, 24, 128)
        sums[:, 32:, :] = groups[2][0][...].reshape(256, 8, 128)
    else:
        two.turn()
        one.turn()
        three.combine_wide()
        two.combine_thin()
        one.combine_thin()
        three.turn()
        two.deepen()
        one.deepen()
        three.combine_thin()
        sums[0:8, :] = one.result() * scale
        three.deepen()
        sums[8:27, :] = two.result() * scale
        sums[32:40, :] = three.result() * scale
        one.drain()
        two.drain()
        three.drain()
    store.wait()


VM = pl.BlockSpec(memory_space=pltpu.VMEM)
ANY = pl.BlockSpec(memory_space=pl.ANY)


def shape(dims, kind=F32):
    return jax.ShapeDtypeStruct(dims, kind)


def block_step(inputs, out_grad, conv_first, conv_middle, conv_last, gain, span, scale, alone=False):
    rows = inputs.shape[0]

    def body(*refs):
        kernel(span, scale, alone, *refs)

    def vmem(*dims, kind=F32):
        return pltpu.VMEM(dims, kind)

    dma = pltpu.SemaphoreType.DMA
    scratch = [
        vmem(rows, 1024, kind=BF16), vmem(rows, 1024, kind=BF16), vmem(1024, 256, kind=BF16),
        vmem(2304, 256, kind=BF16), vmem(256, 1024, kind=BF16),
        vmem(rows, 256), vmem(2, rows + 2 * PAD, 128), vmem(2, 2, rows + 2 * PAD, 128),
        vmem(rows, 768, kind=BF16), vmem(rows, 256), vmem(rows, 512, kind=BF16), vmem(rows, 256),
        vmem(256, 256), vmem(256, 128), vmem(256, 1024),
        vmem(16, 17, 128), vmem(16, 17, 128), vmem(16 if alone else 1, 136, 64),
        vmem(16, 17, 128), vmem(16, 17, 128), vmem(16, 17, 128), vmem(16, 17, 128),
        vmem(3, 17, 128), vmem(3, 17, 128),
        vmem(4, 256, 256), vmem(4, 256, 256), vmem(8, 1024),
        vmem(rows, 1024), vmem(rows, 1024), vmem(rows, 1024, kind=BF16), vmem(256, 1024, kind=BF16),
        vmem(256, 1024), vmem(8, 1024), vmem(8, 1024), vmem(256, 1024, kind=BF16),
        vmem(8, 256, 128), vmem(2, 2304, 128), vmem(2, 1024, 128),
        vmem(768, rows, kind=BF16), vmem(256, rows, kind=BF16), vmem(1024, rows, kind=BF16),
        vmem(256, 1024, kind=BF16), vmem(2304, 256, kind=BF16), vmem(1024, 256, kind=BF16),
        vmem(rows, 256, kind=BF16), vmem(rows, 1024, kind=BF16), dma((6,)), *([dma((16,))] * 4 + [dma((1,))] * 2) * 2,
        *(vmem(256 * size, 128) for size in SLOTS),
        *(vmem(8, 4, 4, size, 128) for size in USED), *(vmem(8, 4, 4, size, 128) for size in USED),
        *(vmem(2, 4, 4, size, 128) for size in USED), *(vmem(2, 8, size, 128) for size in USED),
        *(vmem(2, 4, 2, 2, 4, size, 128) for size in USED), *(vmem(2, 4, 2, 2, size, 128) for size in USED[:2]), vmem(2, 4, 4, USED[2], 128),
        *[dma((33,))] * 6,
    ]
    params = {} if alone else dict(collective_id=0, has_side_effects=True)
    return pl.pallas_call(
        body,
        out_shape=(shape((rows, 1024), BF16), shape((256, 40, 128) if alone else (40, 128))),
        in_specs=[ANY] * 5 + [VM],
        out_specs=(ANY, VM),
        scratch_shapes=scratch,
        compiler_params=pltpu.CompilerParams(vmem_limit_bytes=67043328, **params),
        name="block_step",
    )(inputs, out_grad, conv_first, conv_middle, conv_last, gain.reshape(1, -1))


def finish_kernel(source, sums, target, first, middle, last, gain, buffer, small, arrive, leave):
    count = buffer.shape[0]
    size = source.shape[0] // count
    spans = [pl.ds(n * size, size) for n in range(count)]
    into = [pltpu.make_async_copy(source.at[rows], buffer.at[n], arrive.at[n]) for n, rows in enumerate(spans)]
    out = [pltpu.make_async_copy(buffer.at[n], target.at[rows], leave.at[n]) for n, rows in enumerate(spans)]
    into.append(pltpu.make_async_copy(sums, small, arrive.at[count]))
    pieces = ((small.at[32:40], first), (small.at[8:26], middle), (small.at[0:8], last))
    for n, (piece, place) in enumerate(pieces):
        out.append(pltpu.make_async_copy(piece, place, leave.at[count + n]))
    into[count].start()
    for n in range(count):
        into[n].start()
    into[count].wait()
    for n in range(3):
        out[count + n].start()
    gain[...] = small[26:27, :4]
    for n in range(count):
        into[n].wait()
        out[n].start()
    for one in out:
        one.wait()


def finish(input_grad, sums):
    rows, width = input_grad.shape
    count = 2
    dma = pltpu.SemaphoreType.DMA
    return pl.pallas_call(
        finish_kernel,
        out_shape=(
            shape((rows, width), BF16), shape((8, 128)), shape((18, 128)), shape((8, 128)), shape((1, 4))
        ),
        in_specs=[ANY, ANY],
        out_specs=(ANY, ANY, ANY, ANY, VM),
        scratch_shapes=[
            pltpu.VMEM((count, rows // count, width), BF16), pltpu.VMEM((40, 128), F32), dma((count + 1,)),
            dma((count + 3,)),
        ],
        name="finish",
    )(input_grad, sums)


def shards(inputs, out_grad, conv_first, conv_middle, conv_last, gain):
    ghosts, groups = lax.axis_size("ghost"), lax.axis_size("group")
    span = float(inputs.shape[0] * ghosts)
    input_grad, sums = block_step(
        inputs, out_grad, conv_first, conv_middle, conv_last, gain, span, (span * groups) ** (-0.5)
    )
    input_grad, *grads = finish(input_grad, sums)
    return (input_grad, *(grad.reshape(-1) for grad in grads))


def solution(mesh):
    rows = P(("group", "ghost"))
    return jax.shard_map(
        shards,
        mesh=mesh,
        in_specs=(P(("group", "ghost"), None), P(("group", "ghost"), None), P(), P(), P(), P()),
        out_specs=(P(("group", "ghost"), None), rows, rows, rows, rows),
        check_vma=False,
    )
```
